32 devices in a mesh: ctx: 8 (over z, y), head: 4 (over x, core).
Axes of the slice: x: 2, y: 2, z: 4, core: 2. Of those that a mesh axis runs over, the one named last changes fastest.
Arguments:
- tokens: bfloat16 [2048, 6144], P('ctx'), may hold values from -6 to 6
- query_heads: bfloat16 [2048, 4096], P('ctx', 'head'), may hold values from -6 to 6
- key_heads: bfloat16 [2048, 4096], P('ctx', 'head'), may hold values from -6 to 6
- w_value: bfloat16 [6144, 4096], P('ctx', 'head'), may hold values from -0.078125 to 0.078125
- norm_gain: float32 [4096], P('head'), may hold values from 0.5 to 1.5
Outputs:
- attn_out: bfloat16 [2048, 4096], P('ctx', 'head')
The draws below stay inside these ranges and needn't reach their ends.
All inputs are finite; a program needn't handle non-finite values.
Results may differ from the reference program's by a relative error of at most 0.0054.
Values may be sent and summed in bfloat16 or wider, within the bound.
A program may use at most 128 MiB of HBM per device.

```python
import jax
import jax.numpy as jnp
from jax import lax

D = 6144
HEADS = 32
HD = 128
BLOCK = 256
TOKENS = 2048
HC = 4096


def block_levels(key, shape, split, low, high):
    def one(position, shards_of):
        heights = jax.random.uniform(jax.random.fold_in(jax.random.fold_in(key, 6), position), (shards_of,), jnp.float32, low / len(split), high / len(split))
        return jnp.repeat(jnp.exp(heights), shape[position] // shards_of).reshape((-1,) + (1,) * (len(shape) - position - 1))

    gain = one(*split[0])
    for cut in split[1:]:
        gain = gain * one(*cut)
    return gain


def normal_values(key, shape, spread, most, split=(), kind=jnp.bfloat16):
    array = spread * jax.random.normal(key, shape, jnp.float32)
    if split:
        array = array * block_levels(key, shape, split, -0.22, 0.18)
    return jnp.clip(array, -most, most).astype(kind)


def setup_inputs(seed: int = 0) -> dict:
    streams_of = jax.random.split(jax.random.key(seed), 6)
    return {
        "tokens": normal_values(streams_of[0], (TOKENS, D), 1.0, 6.0, ((0, 8),)),
        "query_heads": normal_values(streams_of[1], (TOKENS, HC), 1.0, 6.0, ((0, 8), (1, 4))),
        "key_heads": normal_values(streams_of[2], (TOKENS, HC), 1.0, 6.0, ((0, 8), (1, 4))),
        "w_value": normal_values(streams_of[3], (D, HC), D ** -0.5, 0.078125, ((0, 8), (1, 4))),
        "norm_gain": jnp.clip(1.0 + 0.1 * jax.random.normal(streams_of[4], (HC,), jnp.float32), 0.5, 1.5),
    }


def reference(tokens, query_heads, key_heads, w_value, norm_gain):
    pre_value = jnp.dot(tokens, w_value, preferred_element_type=jnp.float32)
    value_heads = jax.nn.silu(pre_value).astype(jnp.bfloat16)
    block_count = TOKENS // BLOCK
    shaped_q = query_heads.reshape(block_count, BLOCK, HEADS, HD).astype(jnp.float32)
    shaped_k = key_heads.reshape(block_count, BLOCK, HEADS, HD).astype(jnp.float32)
    shaped_v = value_heads.reshape(block_count, BLOCK, HEADS, HD).astype(jnp.float32)
    causal = jnp.tril(jnp.ones((BLOCK, BLOCK), jnp.bool_))

    def one_block(carried, inputs):
        block_q, block_k, block_v = inputs
        inter = jnp.einsum('shd,hde->she', block_q, carried, precision=lax.Precision.HIGHEST)
        scores = jnp.einsum('shd,thd->hst', block_q, block_k, precision=lax.Precision.HIGHEST)
        scores = jnp.where(causal[None], scores, jnp.float32(0.0)).astype(jnp.bfloat16)
        intra = jnp.einsum('hst,thd->shd', scores.astype(jnp.float32), block_v, precision=lax.Precision.HIGHEST)
        local_state = jnp.einsum('shd,she->hde', block_k, block_v, precision=lax.Precision.HIGHEST)
        return (carried + local_state, inter + intra)
    initial = jnp.zeros((HEADS, HD, HD), jnp.float32)
    _, attended = lax.scan(one_block, initial, (shaped_q, shaped_k, shaped_v))
    attended = attended.reshape(TOKENS, HEADS, HD)
    mean_square = lax.optimization_barrier(jnp.mean(attended * attended, axis=2, keepdims=True))
    normed = attended * lax.rsqrt(mean_square + 1e-05) * norm_gain.reshape(1, HEADS, HD)
    return normed.reshape(TOKENS, HEADS * HD).astype(jnp.bfloat16)
```

```python
import functools

import jax
import jax.numpy as jnp
from jax import lax
from jax.experimental import pallas as pl
from jax.experimental.pallas import tpu as pltpu
from jax.sharding import PartitionSpec as P

MESH = pl.DeviceIdType.MESH
F32 = jnp.float32
BF16 = jnp.bfloat16
ORDER = (1, 3, 2)
WIDTHS = (256, 256, 256, 128, 128)
DIRECT = (4,)
PIECES = 4
EDGE = (
    ("score", 0), ("arrive", 20), ("arrive", 30), ("arrive", 21), ("arrive", 31), ("cross", 20), ("cross", 30),
    ("late", 0), ("arrive", 22), ("arrive", 32), ("cross", 21), ("cross", 31), ("arrive", 23), ("arrive", 33),
    ("cross", 22), ("cross", 32), ("arrive", 10), ("arrive", 11), ("cross", 23), ("cross", 33), ("away", 0),
    ("arrive", 12), ("arrive", 13), ("cross", 10), ("cross", 11), ("cross", 12), ("cross", 13), ("near", 0),
    ("own", 0), ("away", 1), ("near", 1), ("own", 1), ("away", 2), ("near", 2), ("own", 2), ("values", 0),
    ("pair", 0), ("away", 3), ("near", 3), ("own", 3), ("values", 1), ("pair", 1), ("away", 4), ("near", 4),
    ("own", 4), ("values", 2), ("row", 0), ("pair", 2), ("row", 1), ("values", 3), ("earlier", 0),
    ("earlier", 1), ("row", 2), ("pair", 3), ("values", 4), ("row", 3), ("finish", 0), ("finish", 1),
    ("earlier", 2), ("earlier", 3), ("earlier", 4), ("finish", 2), ("finish", 3), ("finish", 4),
)
INNER = (
    ("score", 0), ("arrive", 10), ("arrive", 11), ("cross", 10), ("arrive", 12), ("late", 0), ("cross", 11),
    ("arrive", 13), ("cross", 12), ("arrive", 20), ("arrive", 30), ("cross", 13), ("arrive", 21), ("arrive", 31),
    ("cross", 20), ("cross", 30), ("arrive", 22), ("arrive", 32), ("cross", 21), ("cross", 31), ("arrive", 23),
    ("arrive", 33), ("cross", 22), ("cross", 32), ("near", 0), ("cross", 23), ("cross", 33), ("near", 1),
    ("away", 0), ("merge", 0), ("own", 0), ("away", 1), ("own", 1), ("merge", 1), ("near", 2), ("away", 2),
    ("own", 2), ("values", 0), ("merge", 2), ("pair", 0), ("near", 3), ("away", 3), ("own", 3), ("values", 1),
    ("merge", 3), ("row", 0), ("pair", 1), ("near", 4), ("away", 4), ("own", 4), ("values", 2), ("row", 1),
    ("merge", 4), ("pair", 2), ("earlier", 0), ("values", 3), ("earlier", 1), ("row", 2), ("pair", 3),
    ("values", 4), ("row", 3), ("finish", 0), ("finish", 1), ("earlier", 2), ("earlier", 3), ("earlier", 4),
    ("finish", 2), ("finish", 3), ("finish", 4),
)

HD = 128
BLOCK = 256


def prefix(part, axis, combine, identity):
    place = lax.axis_index(axis)
    gathered = lax.all_gather(part, axis)
    state = jnp.zeros_like(part) + jnp.asarray(identity, part.dtype)

    def one(lap, state):
        return combine(state, lax.dynamic_index_in_dim(gathered, lap, 0, False))

    return lax.fori_loop(0, place, one, state)


def add_states(earlier, later):
    return earlier + later


def plain(tokens, query_heads, key_heads, w_value, norm_gain):
    token_count = tokens.shape[0]
    width = w_value.shape[1]
    heads_here = width // HD
    full_weight = lax.all_gather(w_value, "ctx", axis=0, tiled=True)
    pre_value = jnp.dot(tokens, full_weight, preferred_element_type=jnp.float32)
    value_heads = jax.nn.silu(pre_value).astype(jnp.bfloat16)
    block_count = token_count // BLOCK
    block_shape = (block_count, BLOCK, heads_here, HD)
    shaped_q = query_heads.reshape(block_shape)
    shaped_k = key_heads.reshape(block_shape)
    shaped_v = value_heads.reshape(block_shape)
    local_states = jnp.einsum(
        "bshd,bshe->bhde", shaped_k, shaped_v, preferred_element_type=jnp.float32
    )
    device_state = jnp.sum(local_states, axis=0)
    running_sum = jnp.cumsum(local_states, axis=0)
    before_block = jnp.concatenate([jnp.zeros_like(local_states), running_sum[:-1]], axis=0)
    earlier = prefix(device_state, "ctx", add_states, jnp.zeros_like(device_state))
    prefix_state = earlier[None] + before_block
    inter = jnp.einsum(
        "bshd,bhde->bshe",
        shaped_q.astype(jnp.float32),
        prefix_state,
        precision=lax.Precision.HIGHEST,
    )
    scores = jnp.einsum("bshd,bthd->bhst", shaped_q, shaped_k, preferred_element_type=jnp.float32)
    causal = jnp.tril(jnp.ones((BLOCK, BLOCK), jnp.bool_))
    scores = jnp.where(causal[None, None], scores, jnp.float32(0.0)).astype(jnp.bfloat16)
    intra = jnp.einsum("bhst,bthd->bshd", scores, shaped_v, preferred_element_type=jnp.float32)
    attended = (inter + intra).reshape(token_count, heads_here, HD)
    mean_square = jnp.mean(attended * attended, axis=2, keepdims=True)
    normed = attended * lax.rsqrt(mean_square + 1e-05) * norm_gain.reshape(1, heads_here, HD)
    return normed.reshape(token_count, width).astype(jnp.bfloat16)


def layout(widths):
    starts = [sum(widths[:j]) for j in range(len(widths))]
    return [(start, width, start // HD, width // HD) for start, width in zip(starts, widths)]


def buffers(nz, rows, depth, width, widths, direct):
    dma = pltpu.SemaphoreType.DMA
    chunks = len(widths)
    found = {
        "tok": pltpu.VMEM((nz, rows, 2 * depth), BF16),
        "query": pltpu.VMEM((rows, width), BF16),
        "key": pltpu.VMEM((rows, width), BF16),
        "gain": pltpu.VMEM((1, width), F32),
        "scores": pltpu.VMEM((width // HD, rows, rows), BF16),
        "att": pltpu.VMEM((width // HD, rows, HD), F32),
    }
    for j, cw in enumerate(widths):
        nh = cw // HD
        found["wbuf", j] = pltpu.VMEM((2 * depth, cw), BF16)
        found["p_send", j] = pltpu.VMEM((3, rows, cw), BF16)
        found["p_recv", j] = pltpu.VMEM((3, rows, cw), BF16)
        found["far", j] = pltpu.VMEM((2, rows, cw), F32)
        found["far_send", j] = pltpu.VMEM((2, rows, cw), BF16)
        found["far_recv", j] = pltpu.VMEM((rows, cw), BF16)
        found["acc", j] = pltpu.VMEM((rows, cw), F32)
        found["value", j] = pltpu.VMEM((rows, cw), BF16)
        if j in direct:
            found["state", j] = pltpu.VMEM((nh, HD, HD), F32)
            found["d_send", j] = pltpu.VMEM((nh, HD, HD), BF16)
            found["d_recv", j] = pltpu.VMEM((nz - 1, nh, HD, HD), BF16)
            found["before", j] = pltpu.VMEM((nh, HD, HD), F32)
            found["e_send", j] = pltpu.VMEM((nh, HD, HD), F32)
            found["e_recv", j] = pltpu.VMEM((nh, HD, HD), F32)
        else:
            half = (nh, HD // 2, HD)
            found["state", j] = pltpu.VMEM((2,) + half, F32)
            found["state_in", j] = pltpu.VMEM(half, F32)
            for name in ("t_send", "u_send", "t_recv", "u_recv"):
                found[name, j] = pltpu.VMEM(half, BF16)
            found["pre_send", j] = pltpu.VMEM(half, F32)
            found["pre", j] = pltpu.VMEM((2,) + half, F32)
    found["local_sem"] = dma((4 + chunks,))
    for name in ("w", "s", "t", "e"):
        found[name + "_ss"] = dma((chunks,))
        found[name + "_rs"] = dma((chunks,))
    for name in ("tok", "x"):
        found[name + "_ss"] = dma((nz, PIECES))
        found[name + "_rs"] = dma((nz, PIECES))
    found["core_ss"] = dma((2, nz, PIECES))
    found["core_rs"] = dma((2, nz, PIECES))
    found["p_ss"] = dma((3, chunks))
    found["p_rs"] = dma((3, chunks))
    found["f_ss"] = dma((2, chunks))
    found["f_rs"] = dma((chunks,))
    found["u_ss"] = dma((nz, chunks))
    found["u_rs"] = dma((chunks,))
    found["d_ss"] = dma((nz, chunks))
    found["d_rs"] = dma((nz, chunks))
    return found


def fused_kernel(nz, widths, direct, names, tokens, query_in, key_in, weight, gain_in, out, *refs):
    b = dict(zip(names, refs, strict=True))
    tok, query, key, gain, scores, att = (b[name] for name in ("tok", "query", "key", "gain", "scores", "att"))
    parts = layout(widths)
    chunks = len(parts)
    ctx = lax.axis_index("ctx")
    head = lax.axis_index("head")
    zi, yi = ctx // 2, ctx % 2
    rows = tokens.shape[0]
    depth = weight.shape[0]
    slice_width = 2 * depth
    piece = rows // (4 * PIECES)

    z_peers = {1: zi + 1 - 2 * (zi % 2), 2: lax.rem(zi + 2, nz), 3: nz - 1 - zi}
    edge = (zi == 0) | (zi == nz - 1)
    inner = (zi != 0) & (zi != nz - 1)

    def device_z(m):
        return (z_peers[m] * 2 + yi, head)

    pair = (zi * 2 + 1 - yi, head)
    core_peer = head + 1 - 2 * (head % 2)
    x_peer = lax.rem(head + 2, 4)

    def remote(src, dst, ss, rs, device):
        return pltpu.make_async_remote_copy(
            src_ref=src, dst_ref=dst, send_sem=ss, recv_sem=rs, device_id=device, device_id_type=MESH
        )

    def columns(z):
        return pl.ds(pl.multiple_of(z * slice_width, 128), slice_width)

    def token_rows(h, q):
        return pl.ds(pl.multiple_of((h * PIECES + q) * piece, piece), piece)

    own_rows = pl.ds(pl.multiple_of(yi * depth, depth), depth)

    barrier = pltpu.get_barrier_semaphore()
    greeted = [device_z(m) for m in z_peers] + [pair, (ctx, core_peer), (ctx, x_peer)]
    for device in greeted:
        pl.semaphore_signal(barrier, inc=1, device_id=device, device_id_type=MESH)

    def local(src, dst, i):
        copy = pltpu.make_async_copy(src, dst, b["local_sem"].at[i])
        copy.start()
        return copy

    loads = [local(query_in, query, 0), local(key_in, key, 1), local(gain_in, gain, 2)]
    own_tokens = local(tokens.at[:, columns(zi)], tok.at[zi], 3)
    own_weights = [
        local(weight.at[:, pl.ds(start, cw)], b["wbuf", j].at[own_rows, :], 4 + j)
        for j, (start, cw, _, _) in enumerate(parts)
    ]

    places = [(m, q) for q in range(PIECES) for m in ORDER]
    token_copies = {
        (m, q): remote(
            tokens.at[token_rows(head, q), columns(z_peers[m])],
            tok.at[zi, token_rows(head, q), :],
            b["tok_ss"].at[m, q], b["tok_rs"].at[m, q], device_z(m),
        )
        for m, q in places
    }
    w_copies = [
        remote(
            weight.at[:, pl.ds(start, cw)], b["wbuf", j].at[own_rows, :], b["w_ss"].at[j], b["w_rs"].at[j], pair
        )
        for j, (start, cw, _, _) in enumerate(parts)
    ]
    x_copies, core_copies = {}, {}
    for m, q in places:
        mine = tok.at[z_peers[m], token_rows(head, q), :]
        other = tok.at[z_peers[m], token_rows(x_peer, q), :]
        x_copies[m, q] = remote(mine, mine, b["x_ss"].at[m, q], b["x_rs"].at[m, q], (ctx, x_peer))
        for i, part in enumerate((mine, other)):
            core_copies[m, q, i] = remote(
                part, part, b["core_ss"].at[i, m, q], b["core_rs"].at[i, m, q], (ctx, core_peer)
            )
    p_copies = {
        (i, j): remote(
            b["p_send", j].at[i], b["p_recv", j].at[i], b["p_ss"].at[i, j], b["p_rs"].at[i, j], device_z(1)
        )
        for i in range(3) for j in range(chunks)
    }
    far_copies = {
        (i, j): remote(
            b["far_send", j].at[i], b["far_recv", j], b["f_ss"].at[i, j], b["f_rs"].at[j], device_z(m)
        )
        for i, m in enumerate((3, 2)) for j in range(chunks)
    }
    tree = [j for j in range(chunks) if j not in direct]
    s_copies = {
        j: remote(b["state", j].at[1 - yi], b["state_in", j], b["s_ss"].at[j], b["s_rs"].at[j], pair) for j in tree
    }
    t_copies = {
        j: remote(b["t_send", j], b["t_recv", j], b["t_ss"].at[j], b["t_rs"].at[j], device_z(1)) for j in tree
    }
    u_copies = {
        (m, j): remote(b["u_send", j], b["u_recv", j], b["u_ss"].at[m, j], b["u_rs"].at[j], device_z(m))
        for m in (2, 3) for j in tree
    }
    e_copies = {
        j: remote(b["pre_send", j], b["pre", j].at[yi], b["e_ss"].at[j], b["e_rs"].at[j], pair) for j in tree
    }
    d_copies = {}
    for j in direct:
        e_copies[j] = remote(b["e_send", j], b["e_recv", j], b["e_ss"].at[j], b["e_rs"].at[j], pair)
        for z in range(1, nz):
            d_copies[z, j] = remote(
                b["d_send", j], b["d_recv", j].at[lax.min(zi, nz - 2)],
                b["d_ss"].at[z, j], b["d_rs"].at[lax.min(zi, nz - 2), j], (z * 2 + yi, head),
            )

    pl.semaphore_wait(barrier, len(greeted))

    for q in range(PIECES):
        token_copies[1, q].start()
        for role, m in ((edge, 3), (inner, 2)):
            pl.when(role)(token_copies[m, q].start)

    for copy in w_copies:
        copy.start()

    done = set()
    outer = [False]

    def once(*what):
        fresh = what not in done
        done.add(what)
        return fresh

    def tokens_of(m):
        if once("tokens", m):
            for q in range(PIECES):
                core_copies[m, q, 0].wait_recv()
                core_copies[m, q, 1].wait_recv()
        return tok[z_peers[m]]

    def weights_of(j):
        if once("weights", j):
            own_weights[j].wait()
            w_copies[j].wait_recv()
        return b["wbuf", j][...]

    def score(_):
        for copy in loads:
            copy.wait()
        row = lax.broadcasted_iota(jnp.int32, (rows, rows), 0)
        column = lax.broadcasted_iota(jnp.int32, (rows, rows), 1)
        causal = column <= row
        for hd in range(scores.shape[0]):
            lanes = pl.ds(hd * HD, HD)
            full = lax.dot_general(
                query[:, lanes], key[:, lanes], (((1,), (1,)), ((), ())), preferred_element_type=F32
            )
            scores[hd] = jnp.where(causal, full, 0.0).astype(BF16)

    def late(_):
        for q in range(PIECES):
            token_copies[2 if outer[0] else 3, q].start()

    def arrive(place):
        m, q = divmod(place, 10)
        token_copies[m, q].wait_recv()
        x_copies[m, q].start()
        core_copies[m, q, 0].start()

    def cross(place):
        m, q = divmod(place, 10)
        x_copies[m, q].wait_recv()
        core_copies[m, q, 1].start()

    def near(j):
        b["p_send", j][0] = jnp.dot(tokens_of(1), weights_of(j), preferred_element_type=F32).astype(BF16)
        p_copies[0, j].start()

    def away(j):
        for i, m in enumerate((3, 2)):
            product = jnp.dot(tokens_of(m), weights_of(j), preferred_element_type=F32)
            if outer[0]:
                b["p_send", j][1 + i] = product.astype(BF16)
                p_copies[1 + i, j].start()
            else:
                b["far", j][i] = product

    def own(j):
        if once("own"):
            own_tokens.wait()
        b["acc", j][...] = jnp.dot(tok[zi], weights_of(j), preferred_element_type=F32)

    def merge(j):
        for i in (1, 0):
            p_copies[2 - i, j].wait_recv()
            b["far_send", j][i] = (b["far", j][i] + b["p_recv", j][2 - i].astype(F32)).astype(BF16)
            far_copies[i, j].start()

    def values(j):
        _, _, first, nh = parts[j]
        p_copies[0, j].wait_recv()
        far_copies[0, j].wait_recv()
        total = b["acc", j][...] + b["p_recv", j][0].astype(F32) + b["far_recv", j][...].astype(F32)
        b["value", j][...] = (total / (1.0 + jnp.exp(-total))).astype(BF16)
        for i in range(nh):
            state = lax.dot_general(
                key[:, pl.ds((first + i) * HD, HD)], b["value", j][:, pl.ds(i * HD, HD)],
                (((0,), (0,)), ((), ())), preferred_element_type=F32,
            )
            if j in direct:
                b["state", j][i] = state
                b["d_send", j][i] = state.astype(BF16)
            else:
                b["state", j][0, i] = state[: HD // 2]
                b["state", j][1, i] = state[HD // 2 :]
        if j in direct:
            for z in range(nz - 1, 0, -1):
                pl.when(zi < z)(d_copies[z, j].start)
        else:
            s_copies[j].start()
        for i in range(nh):
            att[first + i] = jnp.dot(
                scores[first + i], b["value", j][:, pl.ds(i * HD, HD)], preferred_element_type=F32
            )

    def pair_sum(j):
        s_copies[j].wait_recv()
        b["pre_send", j][...] = jnp.zeros(b["pre_send", j].shape, F32)

        @pl.when(zi % 2 == 0)
        def _():
            b["t_send", j][...] = (b["state", j][yi] + b["state_in", j][...]).astype(BF16)
            t_copies[j].start()

    def row_sum(j):
        @pl.when(zi % 2 == 1)
        def _():
            t_copies[j].wait_recv()
            b["pre_send", j][...] = b["t_recv", j][...].astype(F32)

        @pl.when(zi == 1)
        def _():
            total = b["pre_send", j][...] + b["state", j][yi] + b["state_in", j][...]
            b["u_send", j][...] = total.astype(BF16)
            u_copies[3, j].start()
            u_copies[2, j].start()

    def earlier(j):
        second = yi.astype(F32)
        if j in direct:
            b["before", j][...] = jnp.zeros(b["before", j].shape, F32)
            for z in range(nz - 1):
                @pl.when(zi > z)
                def _():
                    remote(
                        b["d_send", j], b["d_recv", j].at[z], b["d_ss"].at[z + 1, j], b["d_rs"].at[z, j], pair
                    ).wait_recv()
                    b["before", j][...] = b["before", j][...] + b["d_recv", j][z].astype(F32)

            b["e_send", j][...] = b["before", j][...] + (1.0 - second) * b["state", j][...]
            e_copies[j].start()
            _, _, first, nh = parts[j]
            for i in range(nh):
                att[first + i] = att[first + i] + exact(first + i, b["before", j][i])
            return

        @pl.when(zi >= 2)
        def _():
            u_copies[2, j].wait_recv()
            b["pre_send", j][...] = b["pre_send", j][...] + b["u_recv", j][...].astype(F32)

        before = b["pre_send", j][...]
        b["pre", j][yi] = before + second * b["state_in", j][...]
        b["pre_send", j][...] = before + (1.0 - second) * b["state", j][yi]
        e_copies[j].start()

    def exact(hd, whole):
        high = whole.astype(BF16)
        low = (whole - high.astype(F32)).astype(BF16)
        q = query[:, pl.ds(hd * HD, HD)]
        return jnp.dot(q, high, preferred_element_type=F32) + jnp.dot(q, low, preferred_element_type=F32)

    def finish(j):
        _, _, first, nh = parts[j]
        e_copies[j].wait_recv()
        for i in range(nh):
            lanes = pl.ds((first + i) * HD, HD)
            if j in direct:
                whole = b["e_recv", j][i]
            else:
                whole = jnp.concatenate([b["pre", j][0, i], b["pre", j][1, i]], axis=0)
            attended = att[first + i] + exact(first + i, whole)
            mean_square = jnp.mean(attended * attended, axis=1, keepdims=True)
            out[:, lanes] = (attended * lax.rsqrt(mean_square + 1e-05) * gain[:, lanes]).astype(BF16)

    stages = {
        "score": score, "late": late, "arrive": arrive, "cross": cross, "near": near, "away": away, "own": own,
        "merge": merge, "values": values, "pair": pair_sum, "row": row_sum, "earlier": earlier, "finish": finish,
    }
    def perform(steps, at_edge):
        done.clear()
        outer[0] = at_edge
        for name, j in steps:
            stages[name](j)

    pl.when(edge)(functools.partial(perform, EDGE, True))
    pl.when(inner)(functools.partial(perform, INNER, False))

    for copy in [*token_copies.values(), *w_copies, *x_copies.values(), *core_copies.values()]:
        copy.wait_send()
    for copy in [*s_copies.values(), *e_copies.values()]:
        copy.wait_send()
    for j in range(chunks):
        p_copies[0, j].wait_send()

    @pl.when(edge)
    def _():
        for j in range(chunks):
            p_copies[1, j].wait_send()
            p_copies[2, j].wait_send()

    @pl.when(inner)
    def _():
        for copy in far_copies.values():
            copy.wait_send()

    @pl.when(zi % 2 == 0)
    def _():
        for copy in t_copies.values():
            copy.wait_send()

    @pl.when(zi == 1)
    def _():
        for copy in u_copies.values():
            copy.wait_send()

    for (z, j), copy in d_copies.items():
        pl.when(zi < z)(copy.wait_send)


def fused(n, tokens, query, key, weight, gain):
    rows = tokens.shape[0]
    depth, width = weight.shape
    nz = n // 2
    hbm = pl.BlockSpec(memory_space=pltpu.HBM)
    found = buffers(nz, rows, depth, width, WIDTHS, DIRECT)
    return pl.pallas_call(
        functools.partial(fused_kernel, nz, WIDTHS, DIRECT, list(found)),
        out_shape=jax.ShapeDtypeStruct((rows, width), BF16),
        in_specs=[hbm] * 5,
        out_specs=pl.BlockSpec(memory_space=pltpu.VMEM),
        scratch_shapes=list(found.values()),
        compiler_params=pltpu.CompilerParams(
            collective_id=0, has_side_effects=True, vmem_limit_bytes=63 << 20
        ),
    )(tokens, query, key, weight, gain.reshape(1, width))


def on_device(n, heads, tokens, query_heads, key_heads, w_value, norm_gain):
    rows = tokens.shape[0]
    depth, width = w_value.shape
    fits = n == 8 and heads == 4 and rows == BLOCK and depth % 128 == 0 and width == sum(WIDTHS)
    if fits:
        return fused(n, tokens, query_heads, key_heads, w_value, norm_gain)
    return plain(tokens, query_heads, key_heads, w_value, norm_gain)


def solution(mesh):
    return jax.shard_map(
        functools.partial(on_device, mesh.shape["ctx"], mesh.shape["head"]),
        mesh=mesh,
        in_specs=(P("ctx", None), P("ctx", "head"), P("ctx", "head"), P("ctx", "head"), P("head")),
        out_specs=P("ctx", "head"),
        check_vma=False,
    )
```

```python
import functools
import types

import jax
import jax.numpy as jnp
from jax import lax
from jax.experimental import pallas as pl
from jax.experimental.pallas import tpu as pltpu
from jax.sharding import PartitionSpec as P

MESH = pl.DeviceIdType.MESH
F32 = jnp.float32
BF16 = jnp.bfloat16
ORDER = (1, 3, 2)
WIDTHS = (256, 256, 256, 128, 128)
DIRECT = (4,)
PIECES = 4
SCORE, LATE, ARRIVE, CROSS, NEAR, AWAY, OWN, MERGE, VALUES, PAIR, ROW, EARLIER, FINISH, HALF = range(14)
EDGE = (
    (SCORE, 0), (ARRIVE, 20), (ARRIVE, 30), (ARRIVE, 21), (ARRIVE, 31), (CROSS, 20), (CROSS, 30), (LATE, 0),
    (ARRIVE, 22), (ARRIVE, 32), (CROSS, 21), (CROSS, 31), (ARRIVE, 23), (ARRIVE, 33), (HALF, 0), (CROSS, 22),
    (CROSS, 32), (ARRIVE, 10), (ARRIVE, 11), (CROSS, 23), (CROSS, 33), (HALF, 1), (ARRIVE, 12), (ARRIVE, 13),
    (CROSS, 10), (CROSS, 11), (CROSS, 12), (CROSS, 13), (NEAR, 0), (OWN, 0), (AWAY, 1), (NEAR, 1), (OWN, 1),
    (AWAY, 2), (NEAR, 2), (OWN, 2), (VALUES, 0), (PAIR, 0), (AWAY, 3), (NEAR, 3), (OWN, 3), (VALUES, 1),
    (PAIR, 1), (AWAY, 4), (NEAR, 4), (OWN, 4), (VALUES, 2), (ROW, 0), (PAIR, 2), (ROW, 1), (VALUES, 3),
    (EARLIER, 0), (EARLIER, 1), (ROW, 2), (PAIR, 3), (VALUES, 4), (ROW, 3), (FINISH, 0), (FINISH, 1),
    (EARLIER, 2), (EARLIER, 3), (EARLIER, 4), (FINISH, 2), (FINISH, 3), (FINISH, 4),
)
INNER = (
    (SCORE, 0), (ARRIVE, 10), (ARRIVE, 11), (CROSS, 10), (ARRIVE, 12), (LATE, 0), (CROSS, 11), (ARRIVE, 13),
    (CROSS, 12), (ARRIVE, 20), (ARRIVE, 30), (CROSS, 13), (ARRIVE, 21), (ARRIVE, 31), (CROSS, 20), (CROSS, 30),
    (ARRIVE, 22), (ARRIVE, 32), (CROSS, 21), (CROSS, 31), (ARRIVE, 23), (ARRIVE, 33), (CROSS, 22), (CROSS, 32),
    (NEAR, 0), (CROSS, 23), (CROSS, 33), (NEAR, 1), (AWAY, 0), (MERGE, 0), (OWN, 0), (AWAY, 1), (OWN, 1),
    (MERGE, 1), (NEAR, 2), (AWAY, 2), (OWN, 2), (VALUES, 0), (MERGE, 2), (PAIR, 0), (NEAR, 3), (AWAY, 3),
    (OWN, 3), (VALUES, 1), (MERGE, 3), (ROW, 0), (PAIR, 1), (NEAR, 4), (AWAY, 4), (OWN, 4), (VALUES, 2),
    (ROW, 1), (MERGE, 4), (PAIR, 2), (EARLIER, 0), (VALUES, 3), (EARLIER, 1), (ROW, 2), (PAIR, 3), (VALUES, 4),
    (ROW, 3), (FINISH, 0), (FINISH, 1), (EARLIER, 2), (EARLIER, 3), (EARLIER, 4), (FINISH, 2), (FINISH, 3),
    (FINISH, 4),
)

HD = 128
BLOCK = 256


def prefix(part, axis, combine, identity):
    place = lax.axis_index(axis)
    gathered = lax.all_gather(part, axis)
    state = jnp.zeros_like(part) + jnp.asarray(identity, part.dtype)

    def one(lap, state):
        return combine(state, lax.dynamic_index_in_dim(gathered, lap, 0, False))

    return lax.fori_loop(0, place, one, state)


def add_states(earlier, later):
    return earlier + later


def plain(tokens, query_heads, key_heads, w_value, norm_gain):
    token_count = tokens.shape[0]
    width = w_value.shape[1]
    heads_here = width // HD
    full_weight = lax.all_gather(w_value, "ctx", axis=0, tiled=True)
    pre_value = jnp.dot(tokens, full_weight, preferred_element_type=jnp.float32)
    value_heads = jax.nn.silu(pre_value).astype(jnp.bfloat16)
    block_count = token_count // BLOCK
    block_shape = (block_count, BLOCK, heads_here, HD)
    shaped_q = query_heads.reshape(block_shape)
    shaped_k = key_heads.reshape(block_shape)
    shaped_v = value_heads.reshape(block_shape)
    local_states = jnp.einsum(
        "bshd,bshe->bhde", shaped_k, shaped_v, preferred_element_type=jnp.float32
    )
    device_state = jnp.sum(local_states, axis=0)
    running_sum = jnp.cumsum(local_states, axis=0)
    before_block = jnp.concatenate([jnp.zeros_like(local_states), running_sum[:-1]], axis=0)
    earlier = prefix(device_state, "ctx", add_states, jnp.zeros_like(device_state))
    prefix_state = earlier[None] + before_block
    inter = jnp.einsum(
        "bshd,bhde->bshe",
        shaped_q.astype(jnp.float32),
        prefix_state,
        precision=lax.Precision.HIGHEST,
    )
    scores = jnp.einsum("bshd,bthd->bhst", shaped_q, shaped_k, preferred_element_type=jnp.float32)
    causal = jnp.tril(jnp.ones((BLOCK, BLOCK), jnp.bool_))
    scores = jnp.where(causal[None, None], scores, jnp.float32(0.0)).astype(jnp.bfloat16)
    intra = jnp.einsum("bhst,bthd->bshd", scores, shaped_v, preferred_element_type=jnp.float32)
    attended = (inter + intra).reshape(token_count, heads_here, HD)
    mean_square = jnp.mean(attended * attended, axis=2, keepdims=True)
    normed = attended * lax.rsqrt(mean_square + 1e-05) * norm_gain.reshape(1, heads_here, HD)
    return normed.reshape(token_count, width).astype(jnp.bfloat16)


def layout(widths):
    starts = [sum(widths[:j]) for j in range(len(widths))]
    return [(start, width, start // HD, width // HD) for start, width in zip(starts, widths)]


def buffers(nz, rows, depth, width, widths, direct):
    chunks = len(widths)

    def dma(*shape):
        return pltpu.SemaphoreType.DMA(shape)

    def each(dtype, *before, skip=()):
        return [None if j in skip else pltpu.VMEM((*before, cw), dtype) for j, cw in enumerate(widths)]

    def states(dtype, *before, size=HD, skip=()):
        return [
            None if j in skip else pltpu.VMEM((*before, cw // HD, size, HD), dtype) for j, cw in enumerate(widths)
        ]

    tree = [j for j in range(chunks) if j not in direct]
    half = functools.partial(states, size=HD // 2, skip=direct)
    whole = functools.partial(states, skip=tree)
    return dict(
        tok=pltpu.VMEM((nz, rows, 2 * depth), BF16),
        query=pltpu.VMEM((rows, width), BF16),
        key=pltpu.VMEM((rows, width), BF16),
        gain=pltpu.VMEM((1, width), F32),
        scores=pltpu.VMEM((width // HD, rows, rows), BF16),
        att=pltpu.VMEM((width // HD, rows, HD), F32),
        wbuf=each(BF16, 2 * depth),
        p_send=each(BF16, 3, rows),
        p_recv=each(BF16, 3, rows),
        far=each(F32, 2, rows),
        far_send=each(BF16, 2, rows),
        far_recv=each(BF16, rows),
        acc=each(F32, rows),
        value=each(BF16, rows),
        state=[a or c for a, c in zip(whole(F32), half(F32, 2))],
        d_send=whole(BF16),
        d_recv=whole(BF16, nz - 1),
        before=whole(F32),
        e_send=whole(F32),
        e_recv=whole(F32),
        state_in=half(F32),
        t_send=half(BF16),
        t_recv=half(BF16),
        u_send=half(BF16),
        u_recv=half(BF16),
        pre_send=half(F32),
        pre=half(F32, 2),
        local_sem=dma(4 + chunks),
        w_ss=dma(chunks), w_rs=dma(chunks),
        s_ss=dma(chunks), s_rs=dma(chunks),
        t_ss=dma(chunks), t_rs=dma(chunks),
        e_ss=dma(chunks), e_rs=dma(chunks),
        tok_ss=dma(nz, PIECES), tok_rs=dma(nz, PIECES),
        x_ss=dma(nz, PIECES), x_rs=dma(nz, PIECES),
        core_ss=dma(2, nz, PIECES), core_rs=dma(2, nz, PIECES),
        p_ss=dma(3, chunks, 2), p_rs=dma(3, chunks, 2),
        f_ss=dma(2, chunks), f_rs=dma(chunks),
        u_ss=dma(nz, chunks), u_rs=dma(chunks),
        d_ss=dma(nz, chunks), d_rs=dma(nz, chunks),
    )


def fused_kernel(nz, widths, direct, place, tokens, query_in, key_in, weight, gain_in, out, *refs):
    b = types.SimpleNamespace(**jax.tree.unflatten(place, refs))
    tok, query, key, gain, scores, att = b.tok, b.query, b.key, b.gain, b.scores, b.att
    parts = layout(widths)
    chunks = len(parts)
    ctx = lax.axis_index("ctx")
    head = lax.axis_index("head")
    zi, yi = ctx // 2, ctx % 2
    rows = tokens.shape[0]
    depth = weight.shape[0]
    slice_width = 2 * depth
    piece = rows // (4 * PIECES)

    z_peers = {1: zi + 1 - 2 * (zi % 2), 2: lax.rem(zi + 2, nz), 3: nz - 1 - zi}
    edge = (zi == 0) | (zi == nz - 1)
    inner = (zi != 0) & (zi != nz - 1)

    def device_z(m):
        return (z_peers[m] * 2 + yi, head)

    pair = (zi * 2 + 1 - yi, head)
    core_peer = head + 1 - 2 * (head % 2)
    x_peer = lax.rem(head + 2, 4)

    def remote(src, dst, ss, rs, device):
        return pltpu.make_async_remote_copy(
            src_ref=src, dst_ref=dst, send_sem=ss, recv_sem=rs, device_id=device, device_id_type=MESH
        )

    def columns(z):
        return pl.ds(pl.multiple_of(z * slice_width, 128), slice_width)

    def token_rows(h, q):
        return pl.ds(pl.multiple_of((q * 4 + h) * piece, piece), piece)

    own_rows = pl.ds(pl.multiple_of(yi * depth, depth), depth)

    barrier = pltpu.get_barrier_semaphore()
    greeted = [device_z(m) for m in z_peers] + [pair, (ctx, core_peer), (ctx, x_peer)]
    for device in greeted:
        pl.semaphore_signal(barrier, inc=1, device_id=device, device_id_type=MESH)

    def local(src, dst, i):
        copy = pltpu.make_async_copy(src, dst, b.local_sem.at[i])
        copy.start()
        return copy

    loads = [local(query_in, query, 0), local(key_in, key, 1), local(gain_in, gain, 2)]
    own_tokens = local(tokens.at[:, columns(zi)], tok.at[zi], 3)
    own_weights = [
        local(weight.at[:, pl.ds(start, cw)], b.wbuf[j].at[own_rows, :], 4 + j)
        for j, (start, cw, _, _) in enumerate(parts)
    ]

    order = [(m, q) for q in range(PIECES) for m in ORDER]
    token_copies = {
        (m, q): remote(
            tokens.at[token_rows(head, q), columns(z_peers[m])],
            tok.at[zi, token_rows(head, q), :],
            b.tok_ss.at[m, q], b.tok_rs.at[m, q], device_z(m),
        )
        for m, q in order
    }
    w_copies = [
        remote(
            weight.at[:, pl.ds(start, cw)], b.wbuf[j].at[own_rows, :], b.w_ss.at[j], b.w_rs.at[j], pair
        )
        for j, (start, cw, _, _) in enumerate(parts)
    ]
    x_copies, core_copies = {}, {}
    for m, q in order:
        mine = tok.at[z_peers[m], token_rows(head, q), :]
        other = tok.at[z_peers[m], token_rows(x_peer, q), :]
        x_copies[m, q] = remote(mine, mine, b.x_ss.at[m, q], b.x_rs.at[m, q], (ctx, x_peer))
        for i, part in enumerate((mine, other)):
            core_copies[m, q, i] = remote(
                part, part, b.core_ss.at[i, m, q], b.core_rs.at[i, m, q], (ctx, core_peer)
            )
    halves = [pl.ds(0, rows // 2), pl.ds(rows // 2, rows // 2)]
    p_copies = {}
    for j in range(chunks):
        for i in range(3):
            cuts = halves if j == 0 and i > 0 else [pl.ds(0, rows)]
            p_copies[i, j] = [
                remote(
                    b.p_send[j].at[i, cut], b.p_recv[j].at[i, cut],
                    b.p_ss.at[i, j, r], b.p_rs.at[i, j, r], device_z(1),
                )
                for r, cut in enumerate(cuts)
            ]
    far_copies = {
        (i, j): remote(
            b.far_send[j].at[i], b.far_recv[j], b.f_ss.at[i, j], b.f_rs.at[j], device_z(m)
        )
        for i, m in enumerate((3, 2)) for j in range(chunks)
    }
    tree = [j for j in range(chunks) if j not in direct]
    s_copies = {
        j: remote(b.state[j].at[1 - yi], b.state_in[j], b.s_ss.at[j], b.s_rs.at[j], pair) for j in tree
    }
    t_copies = {
        j: remote(b.t_send[j], b.t_recv[j], b.t_ss.at[j], b.t_rs.at[j], device_z(1)) for j in tree
    }
    u_copies = {
        (m, j): remote(b.u_send[j], b.u_recv[j], b.u_ss.at[m, j], b.u_rs.at[j], device_z(m))
        for m in (2, 3) for j in tree
    }
    e_copies = {
        j: remote(b.pre_send[j], b.pre[j].at[yi], b.e_ss.at[j], b.e_rs.at[j], pair) for j in tree
    }
    d_copies = {}
    for j in direct:
        e_copies[j] = remote(b.e_send[j], b.e_recv[j], b.e_ss.at[j], b.e_rs.at[j], pair)
        for z in range(1, nz):
            d_copies[z, j] = remote(
                b.d_send[j], b.d_recv[j].at[lax.min(zi, nz - 2)],
                b.d_ss.at[z, j], b.d_rs.at[lax.min(zi, nz - 2), j], (z * 2 + yi, head),
            )

    pl.semaphore_wait(barrier, len(greeted))

    for q in range(PIECES):
        token_copies[1, q].start()
        for role, m in ((edge, 3), (inner, 2)):
            pl.when(role)(token_copies[m, q].start)

    for copy in w_copies:
        copy.start()

    done = set()
    outer = [False]

    def once(*what):
        fresh = what not in done
        done.add(what)
        return fresh

    def pieces_of(m, pieces):
        for q in pieces:
            if once("piece", m, q):
                core_copies[m, q, 0].wait_recv()
                core_copies[m, q, 1].wait_recv()

    def tokens_of(m):
        pieces_of(m, range(PIECES))
        return tok[z_peers[m]]

    def weights_of(j):
        if once("weights", j):
            own_weights[j].wait()
            w_copies[j].wait_recv()
        return b.wbuf[j][...]

    def score(_):
        for copy in loads:
            copy.wait()
        row = lax.broadcasted_iota(jnp.int32, (rows, rows), 0)
        column = lax.broadcasted_iota(jnp.int32, (rows, rows), 1)
        causal = column <= row
        for hd in range(scores.shape[0]):
            lanes = pl.ds(hd * HD, HD)
            full = lax.dot_general(
                query[:, lanes], key[:, lanes], (((1,), (1,)), ((), ())), preferred_element_type=F32
            )
            scores[hd] = jnp.where(causal, full, 0.0).astype(BF16)

    def late(_):
        for q in range(PIECES):
            token_copies[2 if outer[0] else 3, q].start()

    def arrive(place):
        m, q = divmod(place, 10)
        token_copies[m, q].wait_recv()
        x_copies[m, q].start()
        core_copies[m, q, 0].start()

    def cross(place):
        m, q = divmod(place, 10)
        x_copies[m, q].wait_recv()
        core_copies[m, q, 1].start()

    def near(j):
        b.p_send[j][0] = jnp.dot(tokens_of(1), weights_of(j), preferred_element_type=F32).astype(BF16)
        p_copies[0, j][0].start()

    def away(j):
        for i, m in enumerate((3, 2)):
            product = jnp.dot(tokens_of(m), weights_of(j), preferred_element_type=F32)
            if outer[0]:
                b.p_send[j][1 + i] = product.astype(BF16)
                for copy in p_copies[1 + i, j]:
                    copy.start()
            else:
                b.far[j][i] = product

    def half(r):
        for i, m in enumerate((3, 2)):
            pieces_of(m, range(r * PIECES // 2, (r + 1) * PIECES // 2))
            block = tok[z_peers[m], r * rows // 2 : (r + 1) * rows // 2, :]
            product = jnp.dot(block, weights_of(0), preferred_element_type=F32)
            b.p_send[0][1 + i, halves[r], :] = product.astype(BF16)
            p_copies[1 + i, 0][r].start()

    def own(j):
        if once("own"):
            own_tokens.wait()
        b.acc[j][...] = jnp.dot(tok[zi], weights_of(j), preferred_element_type=F32)

    def merge(j):
        for i in (1, 0):
            for copy in p_copies[2 - i, j]:
                copy.wait_recv()
            b.far_send[j][i] = (b.far[j][i] + b.p_recv[j][2 - i].astype(F32)).astype(BF16)
            far_copies[i, j].start()

    def values(j):
        _, _, first, nh = parts[j]
        p_copies[0, j][0].wait_recv()
        far_copies[0, j].wait_recv()
        total = b.acc[j][...] + b.p_recv[j][0].astype(F32) + b.far_recv[j][...].astype(F32)
        b.value[j][...] = (total / (1.0 + jnp.exp(-total))).astype(BF16)
        for i in range(nh):
            state = lax.dot_general(
                key[:, pl.ds((first + i) * HD, HD)], b.value[j][:, pl.ds(i * HD, HD)],
                (((0,), (0,)), ((), ())), preferred_element_type=F32,
            )
            if j in direct:
                b.state[j][i] = state
                b.d_send[j][i] = state.astype(BF16)
            else:
                b.state[j][0, i] = state[: HD // 2]
                b.state[j][1, i] = state[HD // 2 :]
        if j in direct:
            for z in range(nz - 1, 0, -1):
                pl.when(zi < z)(d_copies[z, j].start)
        else:
            s_copies[j].start()
        for i in range(nh):
            att[first + i] = jnp.dot(
                scores[first + i], b.value[j][:, pl.ds(i * HD, HD)], preferred_element_type=F32
            )

    def pair_sum(j):
        s_copies[j].wait_recv()
        b.pre_send[j][...] = jnp.zeros(b.pre_send[j].shape, F32)

        @pl.when(zi % 2 == 0)
        def _():
            b.t_send[j][...] = (b.state[j][yi] + b.state_in[j][...]).astype(BF16)
            t_copies[j].start()

    def row_sum(j):
        @pl.when(zi % 2 == 1)
        def _():
            t_copies[j].wait_recv()
            b.pre_send[j][...] = b.t_recv[j][...].astype(F32)

        @pl.when(zi == 1)
        def _():
            total = b.pre_send[j][...] + b.state[j][yi] + b.state_in[j][...]
            b.u_send[j][...] = total.astype(BF16)
            u_copies[3, j].start()
            u_copies[2, j].start()

    def earlier(j):
        second = yi.astype(F32)
        if j in direct:
            b.before[j][...] = jnp.zeros(b.before[j].shape, F32)
            for z in range(nz - 1):
                @pl.when(zi > z)
                def _():
                    remote(
                        b.d_send[j], b.d_recv[j].at[z], b.d_ss.at[z + 1, j], b.d_rs.at[z, j], pair
                    ).wait_recv()
                    b.before[j][...] = b.before[j][...] + b.d_recv[j][z].astype(F32)

            b.e_send[j][...] = b.before[j][...] + (1.0 - second) * b.state[j][...]
            e_copies[j].start()
            _, _, first, nh = parts[j]
            for i in range(nh):
                att[first + i] = att[first + i] + exact(first + i, b.before[j][i])
            return

        @pl.when(zi >= 2)
        def _():
            u_copies[2, j].wait_recv()
            b.pre_send[j][...] = b.pre_send[j][...] + b.u_recv[j][...].astype(F32)

        before = b.pre_send[j][...]
        b.pre[j][yi] = before + second * b.state_in[j][...]
        b.pre_send[j][...] = before + (1.0 - second) * b.state[j][yi]
        e_copies[j].start()

    def exact(hd, whole):
        high = whole.astype(BF16)
        low = (whole - high.astype(F32)).astype(BF16)
        q = query[:, pl.ds(hd * HD, HD)]
        return jnp.dot(q, high, preferred_element_type=F32) + jnp.dot(q, low, preferred_element_type=F32)

    def finish(j):
        _, _, first, nh = parts[j]
        e_copies[j].wait_recv()
        for i in range(nh):
            lanes = pl.ds((first + i) * HD, HD)
            if j in direct:
                whole = b.e_recv[j][i]
            else:
                whole = jnp.concatenate([b.pre[j][0, i], b.pre[j][1, i]], axis=0)
            attended = att[first + i] + exact(first + i, whole)
            mean_square = jnp.mean(attended * attended, axis=1, keepdims=True)
            out[:, lanes] = (attended * lax.rsqrt(mean_square + 1e-05) * gain[:, lanes]).astype(BF16)

    stages = {
        SCORE: score,
        LATE: late,
        ARRIVE: arrive,
        CROSS: cross,
        NEAR: near,
        AWAY: away,
        OWN: own,
        MERGE: merge,
        VALUES: values,
        PAIR: pair_sum,
        ROW: row_sum,
        EARLIER: earlier,
        FINISH: finish,
        HALF: half,
    }

    def perform(steps, at_edge):
        done.clear()
        outer[0] = at_edge
        for stage, j in steps:
            stages[stage](j)

    pl.when(edge)(functools.partial(perform, EDGE, True))
    pl.when(inner)(functools.partial(perform, INNER, False))

    for copy in [*token_copies.values(), *w_copies, *x_copies.values(), *core_copies.values()]:
        copy.wait_send()
    for copy in [*s_copies.values(), *e_copies.values()]:
        copy.wait_send()
    for j in range(chunks):
        p_copies[0, j][0].wait_send()

    @pl.when(edge)
    def _():
        for j in range(chunks):
            for copy in [*p_copies[1, j], *p_copies[2, j]]:
                copy.wait_send()

    @pl.when(inner)
    def _():
        for copy in far_copies.values():
            copy.wait_send()

    @pl.when(zi % 2 == 0)
    def _():
        for copy in t_copies.values():
            copy.wait_send()

    @pl.when(zi == 1)
    def _():
        for copy in u_copies.values():
            copy.wait_send()

    for (z, j), copy in d_copies.items():
        pl.when(zi < z)(copy.wait_send)


def fused(n, tokens, query, key, weight, gain):
    rows = tokens.shape[0]
    depth, width = weight.shape
    nz = n // 2
    hbm = pl.BlockSpec(memory_space=pltpu.HBM)
    scratch, place = jax.tree.flatten(buffers(nz, rows, depth, width, WIDTHS, DIRECT))
    return pl.pallas_call(
        functools.partial(fused_kernel, nz, WIDTHS, DIRECT, place),
        out_shape=jax.ShapeDtypeStruct((rows, width), BF16),
        in_specs=[hbm] * 5,
        out_specs=pl.BlockSpec(memory_space=pltpu.VMEM),
        scratch_shapes=scratch,
        compiler_params=pltpu.CompilerParams(
            collective_id=0, has_side_effects=True, vmem_limit_bytes=63 << 20
        ),
    )(tokens, query, key, weight, gain.reshape(1, width))


def on_device(n, heads, tokens, query_heads, key_heads, w_value, norm_gain):
    rows = tokens.shape[0]
    depth, width = w_value.shape
    fits = n == 8 and heads == 4 and rows == BLOCK and depth % 128 == 0 and width == sum(WIDTHS)
    if fits:
        return fused(n, tokens, query_heads, key_heads, w_value, norm_gain)
    return plain(tokens, query_heads, key_heads, w_value, norm_gain)


def solution(mesh):
    return jax.shard_map(
        functools.partial(on_device, mesh.shape["ctx"], mesh.shape["head"]),
        mesh=mesh,
        in_specs=(P("ctx", None), P("ctx", "head"), P("ctx", "head"), P("ctx", "head"), P("head")),
        out_specs=P("ctx", "head"),
        check_vma=False,
    )
```

```python
import functools
import types

import jax
import jax.numpy as jnp
from jax import lax
from jax.experimental import pallas as pl
from jax.experimental.pallas import tpu as pltpu
from jax.sharding import PartitionSpec as P

MESH = pl.DeviceIdType.MESH
F32 = jnp.float32
BF16 = jnp.bfloat16
ORDER = (1, 3, 2)
WIDTHS = (256, 256, 256, 128, 128)
DIRECT = (4,)
PIECES = 4
SCORE, LATE, ARRIVE, CROSS, NEAR, AWAY, OWN, MERGE, VALUES, PAIR, ROW, EARLIER, FINISH, HALF = range(14)
EDGE = (
    (SCORE, 0), (ARRIVE, 20), (ARRIVE, 30), (ARRIVE, 21), (ARRIVE, 31), (CROSS, 20), (CROSS, 30), (LATE, 0),
    (ARRIVE, 22), (ARRIVE, 32), (CROSS, 21), (CROSS, 31), (ARRIVE, 23), (ARRIVE, 33), (HALF, 0), (CROSS, 22),
    (CROSS, 32), (ARRIVE, 10), (ARRIVE, 11), (CROSS, 23), (CROSS, 33), (HALF, 1), (ARRIVE, 12), (ARRIVE, 13),
    (CROSS, 10), (CROSS, 11), (CROSS, 12), (AWAY, 1), (CROSS, 13), (NEAR, 0), (NEAR, 1), (OWN, 0), (OWN, 1),
    (AWAY, 2), (NEAR, 2), (OWN, 2),
)
INNER = (
    (SCORE, 0), (ARRIVE, 10), (ARRIVE, 11), (CROSS, 10), (ARRIVE, 12), (LATE, 0), (CROSS, 11), (ARRIVE, 13),
    (CROSS, 12), (ARRIVE, 20), (ARRIVE, 30), (CROSS, 13), (ARRIVE, 21), (ARRIVE, 31), (CROSS, 20), (CROSS, 30),
    (ARRIVE, 22), (ARRIVE, 32), (CROSS, 21), (CROSS, 31), (ARRIVE, 23), (ARRIVE, 33), (CROSS, 22), (CROSS, 32),
    (NEAR, 0), (CROSS, 23), (CROSS, 33), (NEAR, 1), (AWAY, 0), (MERGE, 0), (OWN, 0), (AWAY, 1), (OWN, 1),
    (MERGE, 1), (NEAR, 2), (AWAY, 2), (OWN, 2),
)
TAILS = (
    (
        (VALUES, 0), (PAIR, 0), (AWAY, 3), (NEAR, 3), (OWN, 3), (VALUES, 1), (PAIR, 1), (AWAY, 4), (NEAR, 4),
        (OWN, 4), (VALUES, 2), (ROW, 0), (PAIR, 2), (ROW, 1), (VALUES, 3), (EARLIER, 0), (EARLIER, 1), (ROW, 2),
        (PAIR, 3), (VALUES, 4), (ROW, 3), (FINISH, 0), (FINISH, 1), (EARLIER, 2), (EARLIER, 3), (EARLIER, 4),
        (FINISH, 2), (FINISH, 3), (FINISH, 4),
    ),
    (
        (VALUES, 0), (MERGE, 2), (PAIR, 0), (NEAR, 3), (AWAY, 3), (OWN, 3), (VALUES, 1), (MERGE, 3), (ROW, 0),
        (PAIR, 1), (NEAR, 4), (AWAY, 4), (OWN, 4), (VALUES, 2), (ROW, 1), (MERGE, 4), (PAIR, 2), (EARLIER, 0),
        (VALUES, 3), (EARLIER, 1), (ROW, 2), (PAIR, 3), (VALUES, 4), (ROW, 4), (ROW, 3), (FINISH, 0), (FINISH, 1),
        (EARLIER, 2), (EARLIER, 3), (EARLIER, 4), (FINISH, 2), (FINISH, 3), (FINISH, 4),
    ),
    (
        (VALUES, 0), (MERGE, 2), (PAIR, 0), (NEAR, 3), (AWAY, 3), (OWN, 3), (VALUES, 1), (MERGE, 3), (ROW, 0),
        (PAIR, 1), (NEAR, 4), (AWAY, 4), (OWN, 4), (VALUES, 2), (ROW, 1), (MERGE, 4), (PAIR, 2), (EARLIER, 0),
        (VALUES, 3), (EARLIER, 1), (ROW, 2), (PAIR, 3), (VALUES, 4), (ROW, 3), (FINISH, 0), (FINISH, 1),
        (EARLIER, 2), (EARLIER, 3), (EARLIER, 4), (FINISH, 2), (FINISH, 3), (FINISH, 4),
    ),
    (
        (VALUES, 0), (PAIR, 0), (AWAY, 3), (NEAR, 3), (OWN, 3), (VALUES, 1), (PAIR, 1), (AWAY, 4), (NEAR, 4),
        (OWN, 4), (VALUES, 2), (ROW, 0), (PAIR, 2), (ROW, 1), (VALUES, 3), (EARLIER, 0), (EARLIER, 1), (ROW, 2),
        (PAIR, 3), (VALUES, 4), (ROW, 3), (FINISH, 0), (FINISH, 1), (EARLIER, 2), (EARLIER, 3), (EARLIER, 4),
        (FINISH, 2), (FINISH, 3), (FINISH, 4),
    ),
)

HD = 128
BLOCK = 256


def prefix(part, axis, combine, identity):
    place = lax.axis_index(axis)
    gathered = lax.all_gather(part, axis)
    state = jnp.zeros_like(part) + jnp.asarray(identity, part.dtype)

    def one(lap, state):
        return combine(state, lax.dynamic_index_in_dim(gathered, lap, 0, False))

    return lax.fori_loop(0, place, one, state)


def add_states(earlier, later):
    return earlier + later


def plain(tokens, query_heads, key_heads, w_value, norm_gain):
    token_count = tokens.shape[0]
    width = w_value.shape[1]
    heads_here = width // HD
    full_weight = lax.all_gather(w_value, "ctx", axis=0, tiled=True)
    pre_value = jnp.dot(tokens, full_weight, preferred_element_type=jnp.float32)
    value_heads = jax.nn.silu(pre_value).astype(jnp.bfloat16)
    block_count = token_count // BLOCK
    block_shape = (block_count, BLOCK, heads_here, HD)
    shaped_q = query_heads.reshape(block_shape)
    shaped_k = key_heads.reshape(block_shape)
    shaped_v = value_heads.reshape(block_shape)
    local_states = jnp.einsum(
        "bshd,bshe->bhde", shaped_k, shaped_v, preferred_element_type=jnp.float32
    )
    device_state = jnp.sum(local_states, axis=0)
    running_sum = jnp.cumsum(local_states, axis=0)
    before_block = jnp.concatenate([jnp.zeros_like(local_states), running_sum[:-1]], axis=0)
    earlier = prefix(device_state, "ctx", add_states, jnp.zeros_like(device_state))
    prefix_state = earlier[None] + before_block
    inter = jnp.einsum(
        "bshd,bhde->bshe",
        shaped_q.astype(jnp.float32),
        prefix_state,
        precision=lax.Precision.HIGHEST,
    )
    scores = jnp.einsum("bshd,bthd->bhst", shaped_q, shaped_k, preferred_element_type=jnp.float32)
    causal = jnp.tril(jnp.ones((BLOCK, BLOCK), jnp.bool_))
    scores = jnp.where(causal[None, None], scores, jnp.float32(0.0)).astype(jnp.bfloat16)
    intra = jnp.einsum("bhst,bthd->bshd", scores, shaped_v, preferred_element_type=jnp.float32)
    attended = (inter + intra).reshape(token_count, heads_here, HD)
    mean_square = jnp.mean(attended * attended, axis=2, keepdims=True)
    normed = attended * lax.rsqrt(mean_square + 1e-05) * norm_gain.reshape(1, heads_here, HD)
    return normed.reshape(token_count, width).astype(jnp.bfloat16)


def layout(widths):
    starts = [sum(widths[:j]) for j in range(len(widths))]
    return [(start, width, start // HD, width // HD) for start, width in zip(starts, widths)]


def buffers(nz, rows, depth, width, widths, direct):
    chunks = len(widths)

    def dma(*shape):
        return pltpu.SemaphoreType.DMA(shape)

    def each(dtype, *before, skip=()):
        return [None if j in skip else pltpu.VMEM((*before, cw), dtype) for j, cw in enumerate(widths)]

    def states(dtype, *before, size=HD, skip=()):
        return [
            None if j in skip else pltpu.VMEM((*before, cw // HD, size, HD), dtype) for j, cw in enumerate(widths)
        ]

    tree = [j for j in range(chunks) if j not in direct]
    half = functools.partial(states, size=HD // 2, skip=direct)
    whole = functools.partial(states, skip=tree)
    return dict(
        tok=pltpu.VMEM((nz, rows, 2 * depth), BF16),
        query=pltpu.VMEM((rows, width), BF16),
        key=pltpu.VMEM((rows, width), BF16),
        gain=pltpu.VMEM((1, width), F32),
        scores=pltpu.VMEM((width // HD, rows, rows), BF16),
        att=pltpu.VMEM((width // HD, rows, HD), F32),
        wbuf=each(BF16, 2 * depth),
        p_send=each(BF16, 3, rows),
        p_recv=each(BF16, 3, rows),
        far=each(F32, 2, rows),
        far_send=each(BF16, 2, rows),
        far_recv=each(BF16, rows),
        acc=each(F32, rows),
        value=each(BF16, rows),
        state=[a or c for a, c in zip(whole(F32), half(F32, 2))],
        d_send=whole(BF16),
        d_recv=whole(BF16, nz - 1),
        before=whole(F32),
        e_send=[a or c for a, c in zip(whole(BF16), half(BF16))],
        e_recv=[a or c for a, c in zip(whole(BF16), half(BF16))],
        state_out=half(BF16),
        state_in=half(BF16),
        t_send=half(BF16),
        t_recv=half(BF16),
        u_send=half(BF16),
        u_recv=half(BF16),
        pre_send=half(F32),
        pre=half(F32, 2),
        local_sem=dma(4 + chunks),
        w_ss=dma(chunks), w_rs=dma(chunks),
        s_ss=dma(chunks), s_rs=dma(chunks),
        t_ss=dma(chunks), t_rs=dma(chunks),
        e_ss=dma(chunks), e_rs=dma(chunks),
        tok_ss=dma(nz, PIECES), tok_rs=dma(nz, PIECES),
        x_ss=dma(nz, PIECES), x_rs=dma(nz, PIECES),
        core_ss=dma(2, nz, PIECES), core_rs=dma(2, nz, PIECES),
        p_ss=dma(3, chunks, 2), p_rs=dma(3, chunks, 2),
        f_ss=dma(2, chunks), f_rs=dma(chunks),
        u_ss=dma(nz, chunks), u_rs=dma(chunks),
        d_ss=dma(nz, chunks), d_rs=dma(nz, chunks),
    )


def fused_kernel(nz, widths, direct, place, tokens, query_in, key_in, weight, gain_in, out, *refs):
    b = types.SimpleNamespace(**jax.tree.unflatten(place, refs))
    tok, query, key, gain, scores, att = b.tok, b.query, b.key, b.gain, b.scores, b.att
    parts = layout(widths)
    chunks = len(parts)
    ctx = lax.axis_index("ctx")
    head = lax.axis_index("head")
    zi, yi = ctx // 2, ctx % 2
    rows = tokens.shape[0]
    depth = weight.shape[0]
    slice_width = 2 * depth
    piece = rows // (4 * PIECES)

    z_peers = {1: zi + 1 - 2 * (zi % 2), 2: lax.rem(zi + 2, nz), 3: nz - 1 - zi}
    edge = (zi == 0) | (zi == nz - 1)
    inner = (zi != 0) & (zi != nz - 1)

    def device_z(m):
        return (z_peers[m] * 2 + yi, head)

    pair = (zi * 2 + 1 - yi, head)
    core_peer = head + 1 - 2 * (head % 2)
    x_peer = lax.rem(head + 2, 4)

    def remote(src, dst, ss, rs, device):
        return pltpu.make_async_remote_copy(
            src_ref=src, dst_ref=dst, send_sem=ss, recv_sem=rs, device_id=device, device_id_type=MESH
        )

    def columns(z):
        return pl.ds(pl.multiple_of(z * slice_width, 128), slice_width)

    def token_rows(h, q):
        return pl.ds(pl.multiple_of((q * 4 + h) * piece, piece), piece)

    own_rows = pl.ds(pl.multiple_of(yi * depth, depth), depth)

    barrier = pltpu.get_barrier_semaphore()
    greeted = [device_z(m) for m in z_peers] + [pair, (ctx, core_peer), (ctx, x_peer)]
    for device in greeted:
        pl.semaphore_signal(barrier, inc=1, device_id=device, device_id_type=MESH)

    def local(src, dst, i):
        copy = pltpu.make_async_copy(src, dst, b.local_sem.at[i])
        copy.start()
        return copy

    loads = [local(query_in, query, 0), local(key_in, key, 1), local(gain_in, gain, 2)]
    own_tokens = local(tokens.at[:, columns(zi)], tok.at[zi], 3)
    own_weights = [
        local(weight.at[:, pl.ds(start, cw)], b.wbuf[j].at[own_rows, :], 4 + j)
        for j, (start, cw, _, _) in enumerate(parts)
    ]

    order = [(m, q) for q in range(PIECES) for m in ORDER]
    token_copies = {
        (m, q): remote(
            tokens.at[token_rows(head, q), columns(z_peers[m])],
            tok.at[zi, token_rows(head, q), :],
            b.tok_ss.at[m, q], b.tok_rs.at[m, q], device_z(m),
        )
        for m, q in order
    }
    w_copies = [
        remote(
            weight.at[:, pl.ds(start, cw)], b.wbuf[j].at[own_rows, :], b.w_ss.at[j], b.w_rs.at[j], pair
        )
        for j, (start, cw, _, _) in enumerate(parts)
    ]
    x_copies, core_copies = {}, {}
    for m, q in order:
        mine = tok.at[z_peers[m], token_rows(head, q), :]
        other = tok.at[z_peers[m], token_rows(x_peer, q), :]
        x_copies[m, q] = remote(mine, mine, b.x_ss.at[m, q], b.x_rs.at[m, q], (ctx, x_peer))
        for i, part in enumerate((mine, other)):
            core_copies[m, q, i] = remote(
                part, part, b.core_ss.at[i, m, q], b.core_rs.at[i, m, q], (ctx, core_peer)
            )
    halves = [pl.ds(0, rows // 2), pl.ds(rows // 2, rows // 2)]
    p_copies = {}
    for j in range(chunks):
        for i in range(3):
            cuts = halves if j == 0 and i > 0 else [pl.ds(0, rows)]
            p_copies[i, j] = [
                remote(
                    b.p_send[j].at[i, cut], b.p_recv[j].at[i, cut],
                    b.p_ss.at[i, j, r], b.p_rs.at[i, j, r], device_z(1),
                )
                for r, cut in enumerate(cuts)
            ]
    far_copies = {
        (i, j): remote(
            b.far_send[j].at[i], b.far_recv[j], b.f_ss.at[i, j], b.f_rs.at[j], device_z(m)
        )
        for i, m in enumerate((3, 2)) for j in range(chunks)
    }
    tree = [j for j in range(chunks) if j not in direct]
    s_copies = {
        j: remote(b.state_out[j], b.state_in[j], b.s_ss.at[j], b.s_rs.at[j], pair) for j in tree
    }
    t_copies = {
        j: remote(b.t_send[j], b.t_recv[j], b.t_ss.at[j], b.t_rs.at[j], device_z(1))
        for j in tree
    }
    u_copies = {
        (m, j): remote(b.u_send[j], b.u_recv[j], b.u_ss.at[m, j], b.u_rs.at[j], device_z(m))
        for m in (2, 3) for j in tree
    }
    e_copies = {
        j: remote(b.e_send[j], b.e_recv[j], b.e_ss.at[j], b.e_rs.at[j], pair) for j in tree
    }
    d_copies = {}
    for j in direct:
        e_copies[j] = remote(b.e_send[j], b.e_recv[j], b.e_ss.at[j], b.e_rs.at[j], pair)
        for z in range(1, nz):
            d_copies[z, j] = remote(
                b.d_send[j], b.d_recv[j].at[lax.min(zi, nz - 2)],
                b.d_ss.at[z, j], b.d_rs.at[lax.min(zi, nz - 2), j], (z * 2 + yi, head),
            )

    pl.semaphore_wait(barrier, len(greeted))

    for q in range(PIECES):
        token_copies[1, q].start()
        for role, m in ((edge, 3), (inner, 2)):
            pl.when(role)(token_copies[m, q].start)

    for copy in w_copies:
        copy.start()

    done = set()
    outer = [False]

    def once(*what):
        fresh = what not in done
        done.add(what)
        return fresh

    def pieces_of(m, pieces):
        for q in pieces:
            if once("piece", m, q):
                core_copies[m, q, 0].wait_recv()
                core_copies[m, q, 1].wait_recv()

    def tokens_of(m):
        pieces_of(m, range(PIECES))
        return tok[z_peers[m]]

    def weights_of(j):
        if once("weights", j):
            own_weights[j].wait()
            w_copies[j].wait_recv()
        return b.wbuf[j][...]

    def score(_):
        for copy in loads:
            copy.wait()
        row = lax.broadcasted_iota(jnp.int32, (rows, rows), 0)
        column = lax.broadcasted_iota(jnp.int32, (rows, rows), 1)
        causal = column <= row
        for hd in range(scores.shape[0]):
            lanes = pl.ds(hd * HD, HD)
            full = lax.dot_general(
                query[:, lanes], key[:, lanes], (((1,), (1,)), ((), ())), preferred_element_type=F32
            )
            scores[hd] = jnp.where(causal, full, 0.0).astype(BF16)

    def late(_):
        for q in range(PIECES):
            token_copies[2 if outer[0] else 3, q].start()

    def arrive(place):
        m, q = divmod(place, 10)
        token_copies[m, q].wait_recv()
        x_copies[m, q].start()
        core_copies[m, q, 0].start()

    def cross(place):
        m, q = divmod(place, 10)
        x_copies[m, q].wait_recv()
        core_copies[m, q, 1].start()

    def near(j):
        b.p_send[j][0] = jnp.dot(tokens_of(1), weights_of(j), preferred_element_type=F32).astype(BF16)
        p_copies[0, j][0].start()

    def away(j):
        for i, m in enumerate((3, 2)):
            product = jnp.dot(tokens_of(m), weights_of(j), preferred_element_type=F32)
            if outer[0]:
                b.p_send[j][1 + i] = product.astype(BF16)
                for copy in p_copies[1 + i, j]:
                    copy.start()
            else:
                b.far[j][i] = product

    def half(r):
        for i, m in enumerate((3, 2)):
            pieces_of(m, range(r * PIECES // 2, (r + 1) * PIECES // 2))
            block = tok[z_peers[m], r * rows // 2 : (r + 1) * rows // 2, :]
            product = jnp.dot(block, weights_of(0), preferred_element_type=F32)
            b.p_send[0][1 + i, halves[r], :] = product.astype(BF16)
            p_copies[1 + i, 0][r].start()

    def own(j):
        if once("own"):
            own_tokens.wait()
        b.acc[j][...] = jnp.dot(tok[zi], weights_of(j), preferred_element_type=F32)

    def merge(j):
        for i in (1, 0):
            for copy in p_copies[2 - i, j]:
                copy.wait_recv()
            b.far_send[j][i] = (b.far[j][i] + b.p_recv[j][2 - i].astype(F32)).astype(BF16)
            far_copies[i, j].start()

    def values(j):
        _, _, first, nh = parts[j]
        p_copies[0, j][0].wait_recv()
        far_copies[0, j].wait_recv()
        total = b.acc[j][...] + b.p_recv[j][0].astype(F32) + b.far_recv[j][...].astype(F32)
        b.value[j][...] = (total / (1.0 + jnp.exp(-total))).astype(BF16)
        for i in range(nh):
            state = lax.dot_general(
                key[:, pl.ds((first + i) * HD, HD)], b.value[j][:, pl.ds(i * HD, HD)],
                (((0,), (0,)), ((), ())), preferred_element_type=F32,
            )
            if j in direct:
                b.state[j][i] = state
                b.d_send[j][i] = state.astype(BF16)
            else:
                b.state[j][0, i] = state[: HD // 2]
                b.state[j][1, i] = state[HD // 2 :]
        if j in direct:
            b.before[j][...] = jnp.zeros(b.before[j].shape, F32)
            pl.when(zi == 0)(d_copies[1, j].start)
            pl.when(zi == 2)(d_copies[3, j].start)
        else:
            b.state_out[j][...] = b.state[j][1 - yi].astype(BF16)
            s_copies[j].start()
        for i in range(nh):
            att[first + i] = jnp.dot(
                scores[first + i], b.value[j][:, pl.ds(i * HD, HD)], preferred_element_type=F32
            )

    def pair_sum(j):
        s_copies[j].wait_recv()
        b.pre_send[j][...] = jnp.zeros(b.pre_send[j].shape, F32)

        @pl.when(zi % 2 == 0)
        def _():
            b.t_send[j][...] = (b.state[j][yi] + b.state_in[j][...].astype(F32)).astype(BF16)
            t_copies[j].start()

    def landed(j, z):
        remote(
            b.d_send[j], b.d_recv[j].at[z], b.d_ss.at[z + 1, j], b.d_rs.at[z, j], pair
        ).wait_recv()
        b.before[j][...] = b.before[j][...] + b.d_recv[j][z].astype(F32)

    def row_sum(j):
        if j in direct:
            @pl.when(zi == 1)
            def _():
                landed(j, 0)
                b.d_send[j][...] = (b.before[j][...] + b.state[j][...]).astype(BF16)
                d_copies[3, j].start()
                d_copies[2, j].start()

            return
        @pl.when(zi % 2 == 1)
        def _():
            t_copies[j].wait_recv()
            b.pre_send[j][...] = b.t_recv[j][...].astype(F32)

        @pl.when(zi == 1)
        def _():
            total = b.pre_send[j][...] + b.state[j][yi] + b.state_in[j][...].astype(F32)
            b.u_send[j][...] = total.astype(BF16)
            u_copies[3, j].start()
            u_copies[2, j].start()

    def earlier(j):
        second = yi.astype(F32)
        if j in direct:
            pl.when(zi >= 2)(functools.partial(landed, j, 1))
            pl.when(zi == 3)(functools.partial(landed, j, 2))
            b.e_send[j][...] = (b.before[j][...] + (1.0 - second) * b.state[j][...]).astype(BF16)
            e_copies[j].start()
            _, _, first, nh = parts[j]
            for i in range(nh):
                att[first + i] = att[first + i] + exact(first + i, b.before[j][i])
            return

        @pl.when(zi >= 2)
        def _():
            u_copies[2, j].wait_recv()
            b.pre_send[j][...] = b.pre_send[j][...] + b.u_recv[j][...].astype(F32)

        before = b.pre_send[j][...]
        b.pre[j][yi] = before + second * b.state_in[j][...].astype(F32)
        b.e_send[j][...] = (before + (1.0 - second) * b.state[j][yi]).astype(BF16)
        e_copies[j].start()

    def exact(hd, whole):
        high = whole.astype(BF16)
        low = (whole - high.astype(F32)).astype(BF16)
        q = query[:, pl.ds(hd * HD, HD)]
        return jnp.dot(q, high, preferred_element_type=F32) + jnp.dot(q, low, preferred_element_type=F32)

    def finish(j):
        _, _, first, nh = parts[j]
        e_copies[j].wait_recv()
        if j not in direct:
            b.pre[j][1 - yi] = b.e_recv[j][...].astype(F32)
        for i in range(nh):
            lanes = pl.ds((first + i) * HD, HD)
            if j in direct:
                whole = b.e_recv[j][i].astype(F32)
            else:
                whole = jnp.concatenate([b.pre[j][0, i], b.pre[j][1, i]], axis=0)
            attended = att[first + i] + exact(first + i, whole)
            mean_square = jnp.mean(attended * attended, axis=1, keepdims=True)
            out[:, lanes] = (attended * lax.rsqrt(mean_square + 1e-05) * gain[:, lanes]).astype(BF16)

    stages = {
        SCORE: score,
        LATE: late,
        ARRIVE: arrive,
        CROSS: cross,
        NEAR: near,
        AWAY: away,
        OWN: own,
        MERGE: merge,
        VALUES: values,
        PAIR: pair_sum,
        ROW: row_sum,
        EARLIER: earlier,
        FINISH: finish,
        HALF: half,
    }

    def perform(steps):
        for stage, j in steps:
            stages[stage](j)

    def role(steps, at_edge, *places):
        done.clear()
        outer[0] = at_edge
        perform(steps)
        after_head = set(done)
        for z in places:
            done.clear()
            done.update(after_head)
            pl.when(zi == z)(functools.partial(perform, TAILS[z]))

    pl.when(edge)(functools.partial(role, EDGE, True, 0, nz - 1))
    pl.when(inner)(functools.partial(role, INNER, False, 1, nz - 2))

    for copy in [*token_copies.values(), *w_copies, *x_copies.values(), *core_copies.values()]:
        copy.wait_send()
    for copy in [*s_copies.values(), *e_copies.values()]:
        copy.wait_send()
    for j in range(chunks):
        p_copies[0, j][0].wait_send()

    @pl.when(edge)
    def _():
        for j in range(chunks):
            for copy in [*p_copies[1, j], *p_copies[2, j]]:
                copy.wait_send()

    @pl.when(inner)
    def _():
        for copy in far_copies.values():
            copy.wait_send()

    for j, copy in t_copies.items():
        pl.when(zi % 2 == 0)(copy.wait_send)

    @pl.when(zi == 1)
    def _():
        for copy in u_copies.values():
            copy.wait_send()

    for (z, j), copy in d_copies.items():
        pl.when((zi == z - 1) | ((zi == 1) & (z == 3)))(copy.wait_send)


def fused(n, tokens, query, key, weight, gain):
    rows = tokens.shape[0]
    depth, width = weight.shape
    nz = n // 2
    hbm = pl.BlockSpec(memory_space=pltpu.HBM)
    scratch, place = jax.tree.flatten(buffers(nz, rows, depth, width, WIDTHS, DIRECT))
    return pl.pallas_call(
        functools.partial(fused_kernel, nz, WIDTHS, DIRECT, place),
        out_shape=jax.ShapeDtypeStruct((rows, width), BF16),
        in_specs=[hbm] * 5,
        out_specs=pl.BlockSpec(memory_space=pltpu.VMEM),
        scratch_shapes=scratch,
        compiler_params=pltpu.CompilerParams(
            collective_id=0, has_side_effects=True, vmem_limit_bytes=63 << 20
        ),
    )(tokens, query, key, weight, gain.reshape(1, width))


def on_device(n, heads, tokens, query_heads, key_heads, w_value, norm_gain):
    rows = tokens.shape[0]
    depth, width = w_value.shape
    fits = n == 8 and heads == 4 and rows == BLOCK and depth % 128 == 0 and width == sum(WIDTHS)
    if fits:
        return fused(n, tokens, query_heads, key_heads, w_value, norm_gain)
    return plain(tokens, query_heads, key_heads, w_value, norm_gain)


def solution(mesh):
    return jax.shard_map(
        functools.partial(on_device, mesh.shape["ctx"], mesh.shape["head"]),
        mesh=mesh,
        in_specs=(P("ctx", None), P("ctx", "head"), P("ctx", "head"), P("ctx", "head"), P("head")),
        out_specs=P("ctx", "head"),
        check_vma=False,
    )
```

```python
import functools
import types

import jax
import jax.numpy as jnp
from jax import lax
from jax.experimental import pallas as pl
from jax.experimental.pallas import tpu as pltpu
from jax.sharding import PartitionSpec as P

MESH = pl.DeviceIdType.MESH
F32 = jnp.float32
BF16 = jnp.bfloat16
ORDER = (1, 3, 2)
WIDTHS = (256, 256, 256, 128, 128)
DIRECT = (4,)
PIECES = 4
SCORE, LATE, ARRIVE, CROSS, NEAR, AWAY, OWN, MERGE, VALUES, PAIR, ROW, EARLIER, FINISH, HALF = range(14)
EDGE = (
    (SCORE, 0), (ARRIVE, 20), (ARRIVE, 30), (ARRIVE, 21), (ARRIVE, 31), (CROSS, 20), (CROSS, 30), (LATE, 2),
    (ARRIVE, 22), (ARRIVE, 32), (CROSS, 21), (CROSS, 31), (ARRIVE, 23), (ARRIVE, 33), (HALF, 0), (CROSS, 22),
    (CROSS, 32), (ARRIVE, 10), (ARRIVE, 11), (CROSS, 23), (CROSS, 33), (HALF, 1), (ARRIVE, 12), (ARRIVE, 13),
    (CROSS, 10), (CROSS, 11), (CROSS, 12), (AWAY, 1), (CROSS, 13), (NEAR, 0), (NEAR, 1), (OWN, 0), (OWN, 1),
    (AWAY, 2), (NEAR, 2), (OWN, 2), (VALUES, 0), (PAIR, 0), (AWAY, 3), (NEAR, 3), (OWN, 3), (VALUES, 1),
    (PAIR, 1), (AWAY, 4), (NEAR, 4), (OWN, 4), (VALUES, 2), (ROW, 0), (PAIR, 2), (ROW, 1), (VALUES, 3),
    (EARLIER, 0), (EARLIER, 1), (ROW, 2), (PAIR, 3), (VALUES, 4), (ROW, 3), (FINISH, 0), (FINISH, 1),
    (EARLIER, 2), (EARLIER, 3), (EARLIER, 4), (FINISH, 2), (FINISH, 3), (FINISH, 4),
)
INNER = (
    (SCORE, 0), (ARRIVE, 10), (ARRIVE, 11), (LATE, 1), (CROSS, 10), (ARRIVE, 12), (LATE, 3), (CROSS, 11), (ARRIVE, 13),
    (CROSS, 12), (ARRIVE, 20), (ARRIVE, 30), (CROSS, 13), (ARRIVE, 21), (ARRIVE, 31), (CROSS, 20), (CROSS, 30),
    (ARRIVE, 22), (ARRIVE, 32), (CROSS, 21), (CROSS, 31), (ARRIVE, 23), (ARRIVE, 33), (CROSS, 22), (CROSS, 32),
    (NEAR, 0), (CROSS, 23), (CROSS, 33), (NEAR, 1), (AWAY, 0), (MERGE, 0), (OWN, 0), (AWAY, 1), (OWN, 1),
    (MERGE, 1), (NEAR, 2), (AWAY, 2), (OWN, 2), (VALUES, 0), (MERGE, 2), (PAIR, 0), (NEAR, 3), (AWAY, 3),
    (OWN, 3), (VALUES, 1), (MERGE, 3), (ROW, 0), (PAIR, 1), (NEAR, 4), (AWAY, 4), (OWN, 4), (VALUES, 2),
    (ROW, 1), (MERGE, 4), (PAIR, 2), (EARLIER, 0), (VALUES, 3), (EARLIER, 1), (ROW, 2), (PAIR, 3), (VALUES, 4),
    (ROW, 4), (ROW, 3), (FINISH, 0), (FINISH, 1), (EARLIER, 2), (EARLIER, 3), (EARLIER, 4), (FINISH, 2),
    (FINISH, 3), (FINISH, 4),
)

HD = 128
BLOCK = 256


def prefix(part, axis, combine, identity):
    place = lax.axis_index(axis)
    gathered = lax.all_gather(part, axis)
    state = jnp.zeros_like(part) + jnp.asarray(identity, part.dtype)

    def one(lap, state):
        return combine(state, lax.dynamic_index_in_dim(gathered, lap, 0, False))

    return lax.fori_loop(0, place, one, state)


def add_states(earlier, later):
    return earlier + later


def plain(tokens, query_heads, key_heads, w_value, norm_gain):
    token_count = tokens.shape[0]
    width = w_value.shape[1]
    heads_here = width // HD
    full_weight = lax.all_gather(w_value, "ctx", axis=0, tiled=True)
    pre_value = jnp.dot(tokens, full_weight, preferred_element_type=jnp.float32)
    value_heads = jax.nn.silu(pre_value).astype(jnp.bfloat16)
    block_count = token_count // BLOCK
    block_shape = (block_count, BLOCK, heads_here, HD)
    shaped_q = query_heads.reshape(block_shape)
    shaped_k = key_heads.reshape(block_shape)
    shaped_v = value_heads.reshape(block_shape)
    local_states = jnp.einsum(
        "bshd,bshe->bhde", shaped_k, shaped_v, preferred_element_type=jnp.float32
    )
    device_state = jnp.sum(local_states, axis=0)
    running_sum = jnp.cumsum(local_states, axis=0)
    before_block = jnp.concatenate([jnp.zeros_like(local_states), running_sum[:-1]], axis=0)
    earlier = prefix(device_state, "ctx", add_states, jnp.zeros_like(device_state))
    prefix_state = earlier[None] + before_block
    inter = jnp.einsum(
        "bshd,bhde->bshe",
        shaped_q.astype(jnp.float32),
        prefix_state,
        precision=lax.Precision.HIGHEST,
    )
    scores = jnp.einsum("bshd,bthd->bhst", shaped_q, shaped_k, preferred_element_type=jnp.float32)
    causal = jnp.tril(jnp.ones((BLOCK, BLOCK), jnp.bool_))
    scores = jnp.where(causal[None, None], scores, jnp.float32(0.0)).astype(jnp.bfloat16)
    intra = jnp.einsum("bhst,bthd->bshd", scores, shaped_v, preferred_element_type=jnp.float32)
    attended = (inter + intra).reshape(token_count, heads_here, HD)
    mean_square = jnp.mean(attended * attended, axis=2, keepdims=True)
    normed = attended * lax.rsqrt(mean_square + 1e-05) * norm_gain.reshape(1, heads_here, HD)
    return normed.reshape(token_count, width).astype(jnp.bfloat16)


def layout(widths):
    starts = [sum(widths[:j]) for j in range(len(widths))]
    return [(start, width, start // HD, width // HD) for start, width in zip(starts, widths)]


def buffers(nz, rows, depth, width, widths, direct):
    chunks = len(widths)

    def dma(*shape):
        return pltpu.SemaphoreType.DMA(shape)

    def each(dtype, *before, skip=()):
        return [None if j in skip else pltpu.VMEM((*before, cw), dtype) for j, cw in enumerate(widths)]

    def states(dtype, *before, size=HD, skip=()):
        return [
            None if j in skip else pltpu.VMEM((*before, cw // HD, size, HD), dtype) for j, cw in enumerate(widths)
        ]

    tree = [j for j in range(chunks) if j not in direct]
    half = functools.partial(states, size=HD // 2, skip=direct)
    whole = functools.partial(states, skip=tree)
    return dict(
        tok=pltpu.VMEM((nz, rows, 2 * depth), BF16),
        query=pltpu.VMEM((rows, width), BF16),
        key=pltpu.VMEM((rows, width), BF16),
        gain=pltpu.VMEM((1, width), F32),
        scores=pltpu.VMEM((width // HD, rows, rows), BF16),
        att=pltpu.VMEM((width // HD, rows, HD), F32),
        wbuf=each(BF16, 2 * depth),
        p_send=each(BF16, 3, rows),
        p_recv=each(BF16, 3, rows),
        far=each(F32, 2, rows),
        far_send=each(BF16, 2, rows),
        far_recv=each(BF16, rows),
        acc=each(F32, rows),
        value=each(BF16, rows),
        state=[a or c for a, c in zip(whole(F32), half(F32, 2))],
        d_send=whole(BF16),
        d_recv=whole(BF16, nz - 1),
        before=whole(F32),
        e_send=[a or c for a, c in zip(whole(BF16), half(BF16))],
        e_recv=[a or c for a, c in zip(whole(BF16), half(BF16))],
        state_out=half(BF16),
        state_in=half(BF16),
        t_send=half(BF16),
        t_recv=half(BF16),
        u_send=half(BF16),
        u_recv=half(BF16),
        pre_send=half(F32),
        pre=half(F32, 2),
        local_sem=dma(4 + chunks),
        w_ss=dma(chunks), w_rs=dma(chunks),
        s_ss=dma(chunks), s_rs=dma(chunks),
        t_ss=dma(chunks), t_rs=dma(chunks),
        e_ss=dma(chunks), e_rs=dma(chunks),
        tok_ss=dma(nz, PIECES), tok_rs=dma(nz, PIECES),
        x_ss=dma(nz, PIECES), x_rs=dma(nz, PIECES),
        core_ss=dma(2, nz, PIECES), core_rs=dma(2, nz, PIECES),
        p_ss=dma(3, chunks, 2), p_rs=dma(3, chunks, 2),
        f_ss=dma(2, chunks), f_rs=dma(chunks),
        u_ss=dma(nz, chunks), u_rs=dma(chunks),
        d_ss=dma(nz, chunks), d_rs=dma(nz, chunks),
    )


def fused_kernel(nz, widths, direct, place, tokens, query_in, key_in, weight, gain_in, out, *refs):
    b = types.SimpleNamespace(**jax.tree.unflatten(place, refs))
    tok, query, key, gain, scores, att = b.tok, b.query, b.key, b.gain, b.scores, b.att
    parts = layout(widths)
    chunks = len(parts)
    ctx = lax.axis_index("ctx")
    head = lax.axis_index("head")
    zi, yi = ctx // 2, ctx % 2
    rows = tokens.shape[0]
    depth = weight.shape[0]
    slice_width = 2 * depth
    piece = rows // (4 * PIECES)

    z_peers = {1: zi + 1 - 2 * (zi % 2), 2: lax.rem(zi + 2, nz), 3: nz - 1 - zi}
    edge = (zi == 0) | (zi == nz - 1)
    inner = (zi != 0) & (zi != nz - 1)

    def device_z(m):
        return (z_peers[m] * 2 + yi, head)

    pair = (zi * 2 + 1 - yi, head)
    core_peer = head + 1 - 2 * (head % 2)
    x_peer = lax.rem(head + 2, 4)

    def remote(src, dst, ss, rs, device):
        return pltpu.make_async_remote_copy(
            src_ref=src, dst_ref=dst, send_sem=ss, recv_sem=rs, device_id=device, device_id_type=MESH
        )

    def columns(z):
        return pl.ds(pl.multiple_of(z * slice_width, 128), slice_width)

    def token_rows(h, q):
        return pl.ds(pl.multiple_of((q * 4 + h) * piece, piece), piece)

    own_rows = pl.ds(pl.multiple_of(yi * depth, depth), depth)

    barrier = pltpu.get_barrier_semaphore()
    greeted = [device_z(m) for m in z_peers] + [pair, (ctx, core_peer), (ctx, x_peer)]
    for device in greeted:
        pl.semaphore_signal(barrier, inc=1, device_id=device, device_id_type=MESH)

    def local(src, dst, i):
        copy = pltpu.make_async_copy(src, dst, b.local_sem.at[i])
        copy.start()
        return copy

    loads = [local(query_in, query, 0), local(key_in, key, 1), local(gain_in, gain, 2)]
    own_tokens = local(tokens.at[:, columns(zi)], tok.at[zi], 3)
    own_weights = [
        local(weight.at[:, pl.ds(start, cw)], b.wbuf[j].at[own_rows, :], 4 + j)
        for j, (start, cw, _, _) in enumerate(parts)
    ]

    order = [(m, q) for q in range(PIECES) for m in ORDER]
    token_copies = {
        (m, q): remote(
            tokens.at[token_rows(head, q), columns(z_peers[m])],
            tok.at[zi, token_rows(head, q), :],
            b.tok_ss.at[m, q], b.tok_rs.at[m, q], device_z(m),
        )
        for m, q in order
    }
    w_copies = [
        remote(
            weight.at[:, pl.ds(start, cw)], b.wbuf[j].at[own_rows, :], b.w_ss.at[j], b.w_rs.at[j], pair
        )
        for j, (start, cw, _, _) in enumerate(parts)
    ]
    x_copies, core_copies = {}, {}
    for m, q in order:
        mine = tok.at[z_peers[m], token_rows(head, q), :]
        other = tok.at[z_peers[m], token_rows(x_peer, q), :]
        x_copies[m, q] = remote(mine, mine, b.x_ss.at[m, q], b.x_rs.at[m, q], (ctx, x_peer))
        for i, part in enumerate((mine, other)):
            core_copies[m, q, i] = remote(
                part, part, b.core_ss.at[i, m, q], b.core_rs.at[i, m, q], (ctx, core_peer)
            )
    halves = [pl.ds(0, rows // 2), pl.ds(rows // 2, rows // 2)]
    p_copies = {}
    for j in range(chunks):
        for i in range(3):
            cuts = halves if j == 0 and i > 0 else [pl.ds(0, rows)]
            p_copies[i, j] = [
                remote(
                    b.p_send[j].at[i, cut], b.p_recv[j].at[i, cut],
                    b.p_ss.at[i, j, r], b.p_rs.at[i, j, r], device_z(1),
                )
                for r, cut in enumerate(cuts)
            ]
    far_copies = {
        (i, j): remote(
            b.far_send[j].at[i], b.far_recv[j], b.f_ss.at[i, j], b.f_rs.at[j], device_z(m)
        )
        for i, m in enumerate((3, 2)) for j in range(chunks)
    }
    tree = [j for j in range(chunks) if j not in direct]
    s_copies = {
        j: remote(b.state_out[j], b.state_in[j], b.s_ss.at[j], b.s_rs.at[j], pair) for j in tree
    }
    t_copies = {
        j: remote(b.t_send[j], b.t_recv[j], b.t_ss.at[j], b.t_rs.at[j], device_z(1))
        for j in tree
    }
    u_copies = {
        (m, j): remote(b.u_send[j], b.u_recv[j], b.u_ss.at[m, j], b.u_rs.at[j], device_z(m))
        for m in (2, 3) for j in tree
    }
    e_copies = {
        j: remote(b.e_send[j], b.e_recv[j], b.e_ss.at[j], b.e_rs.at[j], pair) for j in tree
    }
    d_copies = {}
    for j in direct:
        e_copies[j] = remote(b.e_send[j], b.e_recv[j], b.e_ss.at[j], b.e_rs.at[j], pair)
        for z in range(1, nz):
            d_copies[z, j] = remote(
                b.d_send[j], b.d_recv[j].at[lax.min(zi, nz - 2)],
                b.d_ss.at[z, j], b.d_rs.at[lax.min(zi, nz - 2), j], (z * 2 + yi, head),
            )

    pl.semaphore_wait(barrier, len(greeted))

    for q in range(PIECES):
        for role, sent in ((edge, (1, 3)), (inner, (2,))):
            for m in sent:
                pl.when(role)(token_copies[m, q].start)

    for copy in w_copies:
        copy.start()

    done = set()
    outer = [False]

    def once(*what):
        fresh = what not in done
        done.add(what)
        return fresh

    def pieces_of(m, pieces):
        for q in pieces:
            if once("piece", m, q):
                core_copies[m, q, 0].wait_recv()
                core_copies[m, q, 1].wait_recv()

    def tokens_of(m):
        pieces_of(m, range(PIECES))
        return tok[z_peers[m]]

    def weights_of(j):
        if once("weights", j):
            own_weights[j].wait()
            w_copies[j].wait_recv()
        return b.wbuf[j][...]

    def score(_):
        for copy in loads:
            copy.wait()
        row = lax.broadcasted_iota(jnp.int32, (rows, rows), 0)
        column = lax.broadcasted_iota(jnp.int32, (rows, rows), 1)
        causal = column <= row
        for hd in range(scores.shape[0]):
            lanes = pl.ds(hd * HD, HD)
            full = lax.dot_general(
                query[:, lanes], key[:, lanes], (((1,), (1,)), ((), ())), preferred_element_type=F32
            )
            scores[hd] = jnp.where(causal, full, 0.0).astype(BF16)

    def late(m):
        for q in range(PIECES):
            token_copies[m, q].start()

    def arrive(place):
        m, q = divmod(place, 10)
        token_copies[m, q].wait_recv()
        x_copies[m, q].start()
        core_copies[m, q, 0].start()

    def cross(place):
        m, q = divmod(place, 10)
        x_copies[m, q].wait_recv()
        core_copies[m, q, 1].start()

    def near(j):
        b.p_send[j][0] = jnp.dot(tokens_of(1), weights_of(j), preferred_element_type=F32).astype(BF16)
        p_copies[0, j][0].start()

    def away(j):
        for i, m in enumerate((3, 2)):
            product = jnp.dot(tokens_of(m), weights_of(j), preferred_element_type=F32)
            if outer[0]:
                b.p_send[j][1 + i] = product.astype(BF16)
                for copy in p_copies[1 + i, j]:
                    copy.start()
            else:
                b.far[j][i] = product

    def half(r):
        for i, m in enumerate((3, 2)):
            pieces_of(m, range(r * PIECES // 2, (r + 1) * PIECES // 2))
            block = tok[z_peers[m], r * rows // 2 : (r + 1) * rows // 2, :]
            product = jnp.dot(block, weights_of(0), preferred_element_type=F32)
            b.p_send[0][1 + i, halves[r], :] = product.astype(BF16)
            p_copies[1 + i, 0][r].start()

    def own(j):
        if once("own"):
            own_tokens.wait()
        b.acc[j][...] = jnp.dot(tok[zi], weights_of(j), preferred_element_type=F32)

    def merge(j):
        for i in (1, 0):
            for copy in p_copies[2 - i, j]:
                copy.wait_recv()
            b.far_send[j][i] = (b.far[j][i] + b.p_recv[j][2 - i].astype(F32)).astype(BF16)
            far_copies[i, j].start()

    def values(j):
        _, _, first, nh = parts[j]
        p_copies[0, j][0].wait_recv()
        far_copies[0, j].wait_recv()
        total = b.acc[j][...] + b.p_recv[j][0].astype(F32) + b.far_recv[j][...].astype(F32)
        b.value[j][...] = (total / (1.0 + jnp.exp(-total))).astype(BF16)
        for i in range(nh):
            state = lax.dot_general(
                key[:, pl.ds((first + i) * HD, HD)], b.value[j][:, pl.ds(i * HD, HD)],
                (((0,), (0,)), ((), ())), preferred_element_type=F32,
            )
            if j in direct:
                b.state[j][i] = state
                b.d_send[j][i] = state.astype(BF16)
            else:
                b.state[j][0, i] = state[: HD // 2]
                b.state[j][1, i] = state[HD // 2 :]
        if j in direct:
            b.before[j][...] = jnp.zeros(b.before[j].shape, F32)
            pl.when(zi == 0)(d_copies[1, j].start)
            pl.when(zi == 2)(d_copies[3, j].start)
        else:
            b.state_out[j][...] = b.state[j][1 - yi].astype(BF16)
            s_copies[j].start()
        for i in range(nh):
            att[first + i] = jnp.dot(
                scores[first + i], b.value[j][:, pl.ds(i * HD, HD)], preferred_element_type=F32
            )

    def pair_sum(j):
        s_copies[j].wait_recv()
        b.pre_send[j][...] = jnp.zeros(b.pre_send[j].shape, F32)

        @pl.when(zi % 2 == 0)
        def _():
            b.t_send[j][...] = (b.state[j][yi] + b.state_in[j][...].astype(F32)).astype(BF16)
            t_copies[j].start()

    def landed(j, z):
        remote(
            b.d_send[j], b.d_recv[j].at[z], b.d_ss.at[z + 1, j], b.d_rs.at[z, j], pair
        ).wait_recv()
        b.before[j][...] = b.before[j][...] + b.d_recv[j][z].astype(F32)

    def row_sum(j):
        if j in direct:
            @pl.when(zi == 1)
            def _():
                landed(j, 0)
                b.d_send[j][...] = (b.before[j][...] + b.state[j][...]).astype(BF16)
                d_copies[3, j].start()
                d_copies[2, j].start()

            return
        @pl.when(zi % 2 == 1)
        def _():
            t_copies[j].wait_recv()
            b.pre_send[j][...] = b.t_recv[j][...].astype(F32)

        @pl.when(zi == 1)
        def _():
            total = b.pre_send[j][...] + b.state[j][yi] + b.state_in[j][...].astype(F32)
            b.u_send[j][...] = total.astype(BF16)
            u_copies[3, j].start()
            u_copies[2, j].start()

    def earlier(j):
        second = yi.astype(F32)
        if j in direct:
            pl.when(zi >= 2)(functools.partial(landed, j, 1))
            pl.when(zi == 3)(functools.partial(landed, j, 2))
            b.e_send[j][...] = (b.before[j][...] + (1.0 - second) * b.state[j][...]).astype(BF16)
            e_copies[j].start()
            _, _, first, nh = parts[j]
            for i in range(nh):
                att[first + i] = att[first + i] + exact(first + i, b.before[j][i])
            return

        @pl.when(zi >= 2)
        def _():
            u_copies[2, j].wait_recv()
            b.pre_send[j][...] = b.pre_send[j][...] + b.u_recv[j][...].astype(F32)

        before = b.pre_send[j][...]
        b.pre[j][yi] = before + second * b.state_in[j][...].astype(F32)
        b.e_send[j][...] = (before + (1.0 - second) * b.state[j][yi]).astype(BF16)
        e_copies[j].start()

    def exact(hd, whole):
        if whole.dtype == BF16:
            return jnp.dot(query[:, pl.ds(hd * HD, HD)], whole, preferred_element_type=F32)

        high = whole.astype(BF16)
        low = (whole - high.astype(F32)).astype(BF16)
        q = query[:, pl.ds(hd * HD, HD)]
        return jnp.dot(q, high, preferred_element_type=F32) + jnp.dot(q, low, preferred_element_type=F32)

    def finish(j):
        _, _, first, nh = parts[j]
        e_copies[j].wait_recv()
        if j not in direct:
            b.pre[j][1 - yi] = b.e_recv[j][...].astype(F32)
        for i in range(nh):
            lanes = pl.ds((first + i) * HD, HD)
            if j in direct:
                whole = b.e_recv[j][i]
            else:
                whole = jnp.concatenate([b.pre[j][0, i], b.pre[j][1, i]], axis=0)
            attended = att[first + i] + exact(first + i, whole)
            mean_square = jnp.mean(attended * attended, axis=1, keepdims=True)
            out[:, lanes] = (attended * lax.rsqrt(mean_square + 1e-05) * gain[:, lanes]).astype(BF16)

    stages = {
        SCORE: score,
        LATE: late,
        ARRIVE: arrive,
        CROSS: cross,
        NEAR: near,
        AWAY: away,
        OWN: own,
        MERGE: merge,
        VALUES: values,
        PAIR: pair_sum,
        ROW: row_sum,
        EARLIER: earlier,
        FINISH: finish,
        HALF: half,
    }

    def perform(steps):
        for stage, j in steps:
            stages[stage](j)

    def role(steps, at_edge):
        done.clear()
        outer[0] = at_edge
        perform(steps)

    pl.when(edge)(functools.partial(role, EDGE, True))
    pl.when(inner)(functools.partial(role, INNER, False))

    for copy in [*token_copies.values(), *w_copies, *x_copies.values(), *core_copies.values()]:
        copy.wait_send()
    for copy in [*s_copies.values(), *e_copies.values()]:
        copy.wait_send()
    for j in range(chunks):
        p_copies[0, j][0].wait_send()

    @pl.when(edge)
    def _():
        for j in range(chunks):
            for copy in [*p_copies[1, j], *p_copies[2, j]]:
                copy.wait_send()

    @pl.when(inner)
    def _():
        for copy in far_copies.values():
            copy.wait_send()

    for j, copy in t_copies.items():
        pl.when(zi % 2 == 0)(copy.wait_send)

    @pl.when(zi == 1)
    def _():
        for copy in u_copies.values():
            copy.wait_send()

    for (z, j), copy in d_copies.items():
        pl.when((zi == z - 1) | ((zi == 1) & (z == 3)))(copy.wait_send)


def fused(n, tokens, query, key, weight, gain):
    rows = tokens.shape[0]
    depth, width = weight.shape
    nz = n // 2
    hbm = pl.BlockSpec(memory_space=pltpu.HBM)
    scratch, place = jax.tree.flatten(buffers(nz, rows, depth, width, WIDTHS, DIRECT))
    return pl.pallas_call(
        functools.partial(fused_kernel, nz, WIDTHS, DIRECT, place),
        out_shape=jax.ShapeDtypeStruct((rows, width), BF16),
        in_specs=[hbm] * 5,
        out_specs=pl.BlockSpec(memory_space=pltpu.VMEM),
        scratch_shapes=scratch,
        compiler_params=pltpu.CompilerParams(
            collective_id=0, has_side_effects=True, vmem_limit_bytes=63 << 20
        ),
    )(tokens, query, key, weight, gain.reshape(1, width))


def on_device(n, heads, tokens, query_heads, key_heads, w_value, norm_gain):
    rows = tokens.shape[0]
    depth, width = w_value.shape
    fits = n == 8 and heads == 4 and rows == BLOCK and depth % 128 == 0 and width == sum(WIDTHS)
    if fits:
        return fused(n, tokens, query_heads, key_heads, w_value, norm_gain)
    return plain(tokens, query_heads, key_heads, w_value, norm_gain)


def solution(mesh):
    return jax.shard_map(
        functools.partial(on_device, mesh.shape["ctx"], mesh.shape["head"]),
        mesh=mesh,
        in_specs=(P("ctx", None), P("ctx", "head"), P("ctx", "head"), P("ctx", "head"), P("head")),
        out_specs=P("ctx", "head"),
        check_vma=False,
    )
```

```python
import functools
import types

import jax
import jax.numpy as jnp
from jax import lax
from jax.experimental import pallas as pl
from jax.experimental.pallas import tpu as pltpu
from jax.sharding import PartitionSpec as P

MESH = pl.DeviceIdType.MESH
F32 = jnp.float32
BF16 = jnp.bfloat16
ORDER = (1, 3, 2)
WIDTHS = (256, 256, 256, 128, 128)
DIRECT = (4,)
PIECES = 4
SCORE, LATE, ARRIVE, CROSS, NEAR, AWAY, OWN, MERGE, VALUES, PAIR, ROW, EARLIER, FINISH, HALF = range(14)
EDGE = (
    (SCORE, 0), (ARRIVE, 20), (ARRIVE, 30), (ARRIVE, 21), (ARRIVE, 31), (CROSS, 20), (CROSS, 30), (LATE, 2),
    (ARRIVE, 22), (ARRIVE, 32), (CROSS, 21), (CROSS, 31), (ARRIVE, 23), (ARRIVE, 33), (HALF, 0), (CROSS, 22),
    (CROSS, 32), (ARRIVE, 10), (ARRIVE, 11), (CROSS, 23), (CROSS, 33), (HALF, 1), (ARRIVE, 12), (ARRIVE, 13),
    (CROSS, 10), (CROSS, 11), (CROSS, 12), (AWAY, 1), (CROSS, 13), (NEAR, 0), (NEAR, 1), (OWN, 0), (OWN, 1),
    (AWAY, 2), (NEAR, 2), (OWN, 2), (VALUES, 0), (PAIR, 0), (AWAY, 3), (NEAR, 3), (OWN, 3), (VALUES, 1),
    (PAIR, 1), (AWAY, 4), (NEAR, 4), (OWN, 4), (VALUES, 2), (ROW, 0), (PAIR, 2), (ROW, 1), (VALUES, 3),
    (EARLIER, 0), (EARLIER, 1), (ROW, 2), (PAIR, 3), (VALUES, 4), (ROW, 3), (FINISH, 0), (FINISH, 1),
    (EARLIER, 2), (EARLIER, 3), (EARLIER, 4), (FINISH, 2), (FINISH, 3), (FINISH, 4),
)
INNER = (
    (SCORE, 0), (ARRIVE, 10), (ARRIVE, 11), (LATE, 1), (CROSS, 10), (ARRIVE, 12), (LATE, 3), (CROSS, 11), (ARRIVE, 13),
    (CROSS, 12), (ARRIVE, 20), (ARRIVE, 30), (CROSS, 13), (ARRIVE, 21), (ARRIVE, 31), (CROSS, 20), (CROSS, 30),
    (ARRIVE, 22), (ARRIVE, 32), (CROSS, 21), (CROSS, 31), (ARRIVE, 23), (ARRIVE, 33), (CROSS, 22), (CROSS, 32),
    (NEAR, 0), (CROSS, 23), (CROSS, 33), (NEAR, 1), (AWAY, 0), (MERGE, 0), (OWN, 0), (AWAY, 1), (OWN, 1),
    (MERGE, 1), (NEAR, 2), (AWAY, 2), (OWN, 2), (VALUES, 0), (MERGE, 2), (PAIR, 0), (NEAR, 3), (AWAY, 3),
    (OWN, 3), (VALUES, 1), (MERGE, 3), (ROW, 0), (PAIR, 1), (NEAR, 4), (AWAY, 4), (OWN, 4), (VALUES, 2),
    (ROW, 1), (MERGE, 4), (PAIR, 2), (EARLIER, 0), (VALUES, 3), (EARLIER, 1), (ROW, 2), (PAIR, 3), (VALUES, 4),
    (ROW, 4), (ROW, 3), (FINISH, 0), (FINISH, 1), (EARLIER, 2), (EARLIER, 3), (EARLIER, 4), (FINISH, 2),
    (FINISH, 3), (FINISH, 4),
)

HD = 128
BLOCK = 256


def prefix(part, axis, combine, identity):
    place = lax.axis_index(axis)
    gathered = lax.all_gather(part, axis)
    state = jnp.zeros_like(part) + jnp.asarray(identity, part.dtype)

    def one(lap, state):
        return combine(state, lax.dynamic_index_in_dim(gathered, lap, 0, False))

    return lax.fori_loop(0, place, one, state)


def add_states(earlier, later):
    return earlier + later


def plain(tokens, query_heads, key_heads, w_value, norm_gain):
    token_count = tokens.shape[0]
    width = w_value.shape[1]
    heads_here = width // HD
    full_weight = lax.all_gather(w_value, "ctx", axis=0, tiled=True)
    pre_value = jnp.dot(tokens, full_weight, preferred_element_type=jnp.float32)
    value_heads = jax.nn.silu(pre_value).astype(jnp.bfloat16)
    block_count = token_count // BLOCK
    block_shape = (block_count, BLOCK, heads_here, HD)
    shaped_q = query_heads.reshape(block_shape)
    shaped_k = key_heads.reshape(block_shape)
    shaped_v = value_heads.reshape(block_shape)
    local_states = jnp.einsum(
        "bshd,bshe->bhde", shaped_k, shaped_v, preferred_element_type=jnp.float32
    )
    device_state = jnp.sum(local_states, axis=0)
    running_sum = jnp.cumsum(local_states, axis=0)
    before_block = jnp.concatenate([jnp.zeros_like(local_states), running_sum[:-1]], axis=0)
    earlier = prefix(device_state, "ctx", add_states, jnp.zeros_like(device_state))
    prefix_state = earlier[None] + before_block
    inter = jnp.einsum(
        "bshd,bhde->bshe",
        shaped_q.astype(jnp.float32),
        prefix_state,
        precision=lax.Precision.HIGHEST,
    )
    scores = jnp.einsum("bshd,bthd->bhst", shaped_q, shaped_k, preferred_element_type=jnp.float32)
    causal = jnp.tril(jnp.ones((BLOCK, BLOCK), jnp.bool_))
    scores = jnp.where(causal[None, None], scores, jnp.float32(0.0)).astype(jnp.bfloat16)
    intra = jnp.einsum("bhst,bthd->bshd", scores, shaped_v, preferred_element_type=jnp.float32)
    attended = (inter + intra).reshape(token_count, heads_here, HD)
    mean_square = jnp.mean(attended * attended, axis=2, keepdims=True)
    normed = attended * lax.rsqrt(mean_square + 1e-05) * norm_gain.reshape(1, heads_here, HD)
    return normed.reshape(token_count, width).astype(jnp.bfloat16)


def layout(widths):
    starts = [sum(widths[:j]) for j in range(len(widths))]
    return [(start, width, start // HD, width // HD) for start, width in zip(starts, widths)]


def buffers(nz, rows, depth, width, widths, direct):
    chunks = len(widths)

    def dma(*shape):
        return pltpu.SemaphoreType.DMA(shape)

    def each(dtype, *before, skip=()):
        return [None if j in skip else pltpu.VMEM((*before, cw), dtype) for j, cw in enumerate(widths)]

    def states(dtype, *before, size=HD, skip=()):
        return [
            None if j in skip else pltpu.VMEM((*before, cw // HD, size, HD), dtype) for j, cw in enumerate(widths)
        ]

    tree = [j for j in range(chunks) if j not in direct]
    half = functools.partial(states, size=HD // 2, skip=direct)
    whole = functools.partial(states, skip=tree)
    return dict(
        tok=pltpu.VMEM((nz, rows, 2 * depth), BF16),
        query=pltpu.VMEM((rows, width), BF16),
        key=pltpu.VMEM((rows, width), BF16),
        gain=pltpu.VMEM((1, width), F32),
        scores=pltpu.VMEM((width // HD, rows, rows), BF16),
        att=pltpu.VMEM((width // HD, rows, HD), F32),
        wbuf=each(BF16, 2 * depth),
        p_send=each(BF16, 3, rows),
        p_recv=each(BF16, 3, rows),
        far=each(F32, 2, rows),
        far_send=each(BF16, 2, rows),
        far_recv=each(BF16, rows),
        acc=each(F32, rows),
        value=each(BF16, rows),
        state=[a or c for a, c in zip(whole(F32), half(F32, 2))],
        d_send=whole(BF16),
        d_recv=whole(BF16, nz - 1),
        before=whole(F32),
        e_send=[a or c for a, c in zip(whole(BF16), half(BF16))],
        e_recv=[a or c for a, c in zip(whole(BF16), half(BF16))],
        state_out=half(BF16),
        state_in=half(BF16),
        t_send=half(BF16),
        t_recv=half(BF16),
        u_send=half(BF16),
        u_recv=half(BF16),
        pre_send=half(F32),
        pre=half(F32, 2),
        local_sem=dma(4 + chunks),
        w_ss=dma(chunks), w_rs=dma(chunks),
        s_ss=dma(chunks), s_rs=dma(chunks),
        t_ss=dma(chunks), t_rs=dma(chunks),
        e_ss=dma(chunks), e_rs=dma(chunks),
        tok_ss=dma(nz, PIECES), tok_rs=dma(nz, PIECES),
        x_ss=dma(nz, PIECES), x_rs=dma(nz, PIECES),
        core_ss=dma(2, nz, PIECES), core_rs=dma(2, nz, PIECES),
        p_ss=dma(3, chunks, 2), p_rs=dma(3, chunks, 2),
        f_ss=dma(2, chunks), f_rs=dma(chunks),
        u_ss=dma(nz, chunks), u_rs=dma(chunks),
        d_ss=dma(nz, chunks), d_rs=dma(nz, chunks),
    )


def fused_kernel(nz, widths, direct, place, tokens, query_in, key_in, weight, gain_in, out, *refs):
    b = types.SimpleNamespace(**jax.tree.unflatten(place, refs))
    tok, query, key, gain, scores, att = b.tok, b.query, b.key, b.gain, b.scores, b.att
    parts = layout(widths)
    chunks = len(parts)
    ctx = lax.axis_index("ctx")
    head = lax.axis_index("head")
    zi, yi = ctx // 2, ctx % 2
    rows = tokens.shape[0]
    depth = weight.shape[0]
    slice_width = 2 * depth
    piece = rows // (4 * PIECES)

    z_peers = {1: zi + 1 - 2 * (zi % 2), 2: lax.rem(zi + 2, nz), 3: nz - 1 - zi}
    edge = (zi == 0) | (zi == nz - 1)
    inner = (zi != 0) & (zi != nz - 1)

    def device_z(m):
        return (z_peers[m] * 2 + yi, head)

    pair = (zi * 2 + 1 - yi, head)
    core_peer = head + 1 - 2 * (head % 2)
    x_peer = lax.rem(head + 2, 4)

    def remote(src, dst, ss, rs, device):
        return pltpu.make_async_remote_copy(
            src_ref=src, dst_ref=dst, send_sem=ss, recv_sem=rs, device_id=device, device_id_type=MESH
        )

    def columns(z):
        return pl.ds(pl.multiple_of(z * slice_width, 128), slice_width)

    def token_rows(h, q):
        return pl.ds(pl.multiple_of((q * 4 + h) * piece, piece), piece)

    own_rows = pl.ds(pl.multiple_of(yi * depth, depth), depth)

    barrier = pltpu.get_barrier_semaphore()
    greeted = [device_z(m) for m in z_peers] + [pair, (ctx, core_peer), (ctx, x_peer)]
    for device in greeted:
        pl.semaphore_signal(barrier, inc=1, device_id=device, device_id_type=MESH)

    def local(src, dst, i):
        copy = pltpu.make_async_copy(src, dst, b.local_sem.at[i])
        copy.start()
        return copy

    loads = [local(query_in, query, 0), local(key_in, key, 1), local(gain_in, gain, 2)]
    own_tokens = local(tokens.at[:, columns(zi)], tok.at[zi], 3)
    own_weights = [
        local(weight.at[:, pl.ds(start, cw)], b.wbuf[j].at[own_rows, :], 4 + j)
        for j, (start, cw, _, _) in enumerate(parts)
    ]

    order = [(m, q) for q in range(PIECES) for m in ORDER]
    token_copies = {
        (m, q): remote(
            tokens.at[token_rows(head, q), columns(z_peers[m])],
            tok.at[zi, token_rows(head, q), :],
            b.tok_ss.at[m, q], b.tok_rs.at[m, q], device_z(m),
        )
        for m, q in order
    }
    w_copies = [
        remote(
            weight.at[:, pl.ds(start, cw)], b.wbuf[j].at[own_rows, :], b.w_ss.at[j], b.w_rs.at[j], pair
        )
        for j, (start, cw, _, _) in enumerate(parts)
    ]
    x_copies, core_copies = {}, {}
    for m, q in order:
        mine = tok.at[z_peers[m], token_rows(head, q), :]
        other = tok.at[z_peers[m], token_rows(x_peer, q), :]
        x_copies[m, q] = remote(mine, mine, b.x_ss.at[m, q], b.x_rs.at[m, q], (ctx, x_peer))
        for i, part in enumerate((mine, other)):
            core_copies[m, q, i] = remote(
                part, part, b.core_ss.at[i, m, q], b.core_rs.at[i, m, q], (ctx, core_peer)
            )
    halves = [pl.ds(0, rows // 2), pl.ds(rows // 2, rows // 2)]
    p_copies = {}
    for j in range(chunks):
        for i in range(3):
            cuts = halves if j == 0 and i > 0 else [pl.ds(0, rows)]
            p_copies[i, j] = [
                remote(
                    b.p_send[j].at[i, cut], b.p_recv[j].at[i, cut],
                    b.p_ss.at[i, j, r], b.p_rs.at[i, j, r], device_z(1),
                )
                for r, cut in enumerate(cuts)
            ]
    far_copies = {
        (i, j): remote(
            b.far_send[j].at[i], b.far_recv[j], b.f_ss.at[i, j], b.f_rs.at[j], device_z(m)
        )
        for i, m in enumerate((3, 2)) for j in range(chunks)
    }
    tree = [j for j in range(chunks) if j not in direct]
    s_copies = {
        j: remote(b.state_out[j], b.state_in[j], b.s_ss.at[j], b.s_rs.at[j], pair) for j in tree
    }
    t_copies = {
        j: remote(b.t_send[j], b.t_recv[j], b.t_ss.at[j], b.t_rs.at[j], device_z(1))
        for j in tree
    }
    u_copies = {
        (m, j): remote(b.u_send[j], b.u_recv[j], b.u_ss.at[m, j], b.u_rs.at[j], device_z(m))
        for m in (2, 3) for j in tree
    }
    e_copies = {
        j: remote(b.e_send[j], b.e_recv[j], b.e_ss.at[j], b.e_rs.at[j], pair) for j in tree
    }
    d_copies = {}
    for j in direct:
        e_copies[j] = remote(b.e_send[j], b.e_recv[j], b.e_ss.at[j], b.e_rs.at[j], pair)
        for z in range(1, nz):
            d_copies[z, j] = remote(
                b.d_send[j], b.d_recv[j].at[lax.min(zi, nz - 2)],
                b.d_ss.at[z, j], b.d_rs.at[lax.min(zi, nz - 2), j], (z * 2 + yi, head),
            )

    pl.semaphore_wait(barrier, len(greeted))

    for q in range(PIECES):
        for role, sent in ((edge, (3, 1)), (inner, (2,))):
            for m in sent:
                pl.when(role)(token_copies[m, q].start)

    for copy in w_copies:
        copy.start()

    done = set()
    outer = [False]

    def once(*what):
        fresh = what not in done
        done.add(what)
        return fresh

    def pieces_of(m, pieces):
        for q in pieces:
            if once("piece", m, q):
                core_copies[m, q, 0].wait_recv()
                core_copies[m, q, 1].wait_recv()

    def tokens_of(m):
        pieces_of(m, range(PIECES))
        return tok[z_peers[m]]

    def weights_of(j):
        if once("weights", j):
            own_weights[j].wait()
            w_copies[j].wait_recv()
        return b.wbuf[j][...]

    def score(_):
        for copy in loads:
            copy.wait()
        row = lax.broadcasted_iota(jnp.int32, (rows, rows), 0)
        column = lax.broadcasted_iota(jnp.int32, (rows, rows), 1)
        causal = column <= row
        for hd in range(scores.shape[0]):
            lanes = pl.ds(hd * HD, HD)
            full = lax.dot_general(
                query[:, lanes], key[:, lanes], (((1,), (1,)), ((), ())), preferred_element_type=F32
            )
            scores[hd] = jnp.where(causal, full, 0.0).astype(BF16)

    def late(m):
        for q in range(PIECES):
            token_copies[m, q].start()

    def arrive(place):
        m, q = divmod(place, 10)
        token_copies[m, q].wait_recv()
        x_copies[m, q].start()
        core_copies[m, q, 0].start()

    def cross(place):
        m, q = divmod(place, 10)
        x_copies[m, q].wait_recv()
        core_copies[m, q, 1].start()

    def near(j):
        b.p_send[j][0] = jnp.dot(tokens_of(1), weights_of(j), preferred_element_type=F32).astype(BF16)
        p_copies[0, j][0].start()

    def away(j):
        for i, m in enumerate((3, 2)):
            product = jnp.dot(tokens_of(m), weights_of(j), preferred_element_type=F32)
            if outer[0]:
                b.p_send[j][1 + i] = product.astype(BF16)
                for copy in p_copies[1 + i, j]:
                    copy.start()
            else:
                b.far[j][i] = product

    def half(r):
        for i, m in enumerate((3, 2)):
            pieces_of(m, range(r * PIECES // 2, (r + 1) * PIECES // 2))
            block = tok[z_peers[m], r * rows // 2 : (r + 1) * rows // 2, :]
            product = jnp.dot(block, weights_of(0), preferred_element_type=F32)
            b.p_send[0][1 + i, halves[r], :] = product.astype(BF16)
            p_copies[1 + i, 0][r].start()

    def own(j):
        if once("own"):
            own_tokens.wait()
        b.acc[j][...] = jnp.dot(tok[zi], weights_of(j), preferred_element_type=F32)

    def merge(j):
        for i in (1, 0):
            for copy in p_copies[2 - i, j]:
                copy.wait_recv()
            b.far_send[j][i] = (b.far[j][i] + b.p_recv[j][2 - i].astype(F32)).astype(BF16)
            far_copies[i, j].start()

    def values(j):
        _, _, first, nh = parts[j]
        p_copies[0, j][0].wait_recv()
        far_copies[0, j].wait_recv()
        total = b.acc[j][...] + b.p_recv[j][0].astype(F32) + b.far_recv[j][...].astype(F32)
        b.value[j][...] = (total / (1.0 + jnp.exp(-total))).astype(BF16)
        for i in range(nh):
            state = lax.dot_general(
                key[:, pl.ds((first + i) * HD, HD)], b.value[j][:, pl.ds(i * HD, HD)],
                (((0,), (0,)), ((), ())), preferred_element_type=F32,
            )
            if j in direct:
                b.state[j][i] = state
                b.d_send[j][i] = state.astype(BF16)
            else:
                b.state[j][0, i] = state[: HD // 2]
                b.state[j][1, i] = state[HD // 2 :]
        if j in direct:
            b.before[j][...] = jnp.zeros(b.before[j].shape, F32)
            pl.when(zi == 0)(d_copies[1, j].start)
            pl.when(zi == 2)(d_copies[3, j].start)
        else:
            b.state_out[j][...] = b.state[j][1 - yi].astype(BF16)
            s_copies[j].start()
        for i in range(nh):
            att[first + i] = jnp.dot(
                scores[first + i], b.value[j][:, pl.ds(i * HD, HD)], preferred_element_type=F32
            )

    def pair_sum(j):
        s_copies[j].wait_recv()
        b.pre_send[j][...] = jnp.zeros(b.pre_send[j].shape, F32)

        @pl.when(zi % 2 == 0)
        def _():
            b.t_send[j][...] = (b.state[j][yi] + b.state_in[j][...].astype(F32)).astype(BF16)
            t_copies[j].start()

    def landed(j, z):
        remote(
            b.d_send[j], b.d_recv[j].at[z], b.d_ss.at[z + 1, j], b.d_rs.at[z, j], pair
        ).wait_recv()
        b.before[j][...] = b.before[j][...] + b.d_recv[j][z].astype(F32)

    def row_sum(j):
        if j in direct:
            @pl.when(zi == 1)
            def _():
                landed(j, 0)
                b.d_send[j][...] = (b.before[j][...] + b.state[j][...]).astype(BF16)
                d_copies[3, j].start()
                d_copies[2, j].start()

            return
        @pl.when(zi % 2 == 1)
        def _():
            t_copies[j].wait_recv()
            b.pre_send[j][...] = b.t_recv[j][...].astype(F32)

        @pl.when(zi == 1)
        def _():
            total = b.pre_send[j][...] + b.state[j][yi] + b.state_in[j][...].astype(F32)
            b.u_send[j][...] = total.astype(BF16)
            u_copies[3, j].start()
            u_copies[2, j].start()

    def earlier(j):
        second = yi.astype(F32)
        if j in direct:
            pl.when(zi >= 2)(functools.partial(landed, j, 1))
            pl.when(zi == 3)(functools.partial(landed, j, 2))
            b.e_send[j][...] = (b.before[j][...] + (1.0 - second) * b.state[j][...]).astype(BF16)
            e_copies[j].start()
            _, _, first, nh = parts[j]
            for i in range(nh):
                att[first + i] = att[first + i] + exact(first + i, b.before[j][i])
            return

        @pl.when(zi >= 2)
        def _():
            u_copies[2, j].wait_recv()
            b.pre_send[j][...] = b.pre_send[j][...] + b.u_recv[j][...].astype(F32)

        before = b.pre_send[j][...]
        b.pre[j][yi] = before + second * b.state_in[j][...].astype(F32)
        b.e_send[j][...] = (before + (1.0 - second) * b.state[j][yi]).astype(BF16)
        e_copies[j].start()

    def exact(hd, whole):
        if whole.dtype == BF16:
            return jnp.dot(query[:, pl.ds(hd * HD, HD)], whole, preferred_element_type=F32)

        high = whole.astype(BF16)
        low = (whole - high.astype(F32)).astype(BF16)
        q = query[:, pl.ds(hd * HD, HD)]
        return jnp.dot(q, high, preferred_element_type=F32) + jnp.dot(q, low, preferred_element_type=F32)

    def finish(j):
        _, _, first, nh = parts[j]
        e_copies[j].wait_recv()
        if j not in direct:
            b.pre[j][1 - yi] = b.e_recv[j][...].astype(F32)
        for i in range(nh):
            lanes = pl.ds((first + i) * HD, HD)
            if j in direct:
                whole = b.e_recv[j][i]
            else:
                whole = jnp.concatenate([b.pre[j][0, i], b.pre[j][1, i]], axis=0)
            attended = att[first + i] + exact(first + i, whole)
            mean_square = jnp.mean(attended * attended, axis=1, keepdims=True)
            out[:, lanes] = (attended * lax.rsqrt(mean_square + 1e-05) * gain[:, lanes]).astype(BF16)

    stages = {
        SCORE: score,
        LATE: late,
        ARRIVE: arrive,
        CROSS: cross,
        NEAR: near,
        AWAY: away,
        OWN: own,
        MERGE: merge,
        VALUES: values,
        PAIR: pair_sum,
        ROW: row_sum,
        EARLIER: earlier,
        FINISH: finish,
        HALF: half,
    }

    def perform(steps):
        for stage, j in steps:
            stages[stage](j)

    def role(steps, at_edge):
        done.clear()
        outer[0] = at_edge
        perform(steps)

    pl.when(edge)(functools.partial(role, EDGE, True))
    pl.when(inner)(functools.partial(role, INNER, False))

    for copy in [*token_copies.values(), *w_copies, *x_copies.values(), *core_copies.values()]:
        copy.wait_send()
    for copy in [*s_copies.values(), *e_copies.values()]:
        copy.wait_send()
    for j in range(chunks):
        p_copies[0, j][0].wait_send()

    @pl.when(edge)
    def _():
        for j in range(chunks):
            for copy in [*p_copies[1, j], *p_copies[2, j]]:
                copy.wait_send()

    @pl.when(inner)
    def _():
        for copy in far_copies.values():
            copy.wait_send()

    for j, copy in t_copies.items():
        pl.when(zi % 2 == 0)(copy.wait_send)

    @pl.when(zi == 1)
    def _():
        for copy in u_copies.values():
            copy.wait_send()

    for (z, j), copy in d_copies.items():
        pl.when((zi == z - 1) | ((zi == 1) & (z == 3)))(copy.wait_send)


def fused(n, tokens, query, key, weight, gain):
    rows = tokens.shape[0]
    depth, width = weight.shape
    nz = n // 2
    hbm = pl.BlockSpec(memory_space=pltpu.HBM)
    scratch, place = jax.tree.flatten(buffers(nz, rows, depth, width, WIDTHS, DIRECT))
    return pl.pallas_call(
        functools.partial(fused_kernel, nz, WIDTHS, DIRECT, place),
        out_shape=jax.ShapeDtypeStruct((rows, width), BF16),
        in_specs=[hbm] * 5,
        out_specs=pl.BlockSpec(memory_space=pltpu.VMEM),
        scratch_shapes=scratch,
        compiler_params=pltpu.CompilerParams(
            collective_id=0, has_side_effects=True, vmem_limit_bytes=63 << 20
        ),
    )(tokens, query, key, weight, gain.reshape(1, width))


def on_device(n, heads, tokens, query_heads, key_heads, w_value, norm_gain):
    rows = tokens.shape[0]
    depth, width = w_value.shape
    fits = n == 8 and heads == 4 and rows == BLOCK and depth % 128 == 0 and width == sum(WIDTHS)
    if fits:
        return fused(n, tokens, query_heads, key_heads, w_value, norm_gain)
    return plain(tokens, query_heads, key_heads, w_value, norm_gain)


def solution(mesh):
    return jax.shard_map(
        functools.partial(on_device, mesh.shape["ctx"], mesh.shape["head"]),
        mesh=mesh,
        in_specs=(P("ctx", None), P("ctx", "head"), P("ctx", "head"), P("ctx", "head"), P("head")),
        out_specs=P("ctx", "head"),
        check_vma=False,
    )
```
